1024 devices in a mesh: slab: 16 (over x, core), dom: 64 (over y, z).
Axes of the slice: x: 8, y: 8, z: 8, core: 2. Of those that a mesh axis runs over, the one named last changes fastest.
Arguments:
- coords: float32 [3, 16, 64, 512], P(None, 'slab', 'dom'), may hold values from -6 to 6
- velocity: float32 [3, 16, 64, 512], P(None, 'slab', 'dom'), may hold values from -6 to 6
- charge: float32 [16, 64, 512], P('slab', 'dom'), may hold values from -1 to 1
- inv_mass: float32 [16, 64, 512], P('slab', 'dom'), may hold values from 0.0625 to 1
- tile_block: int32 [16, 64, 64], P('slab', 'dom'), may hold values from 0 to 3
- tile_atoms: int32 [16, 64, 64, 128], P('slab', 'dom'), may hold values from 0 to 2047
- active_tile_count: int32 [16, 64], P('slab', 'dom'), may hold values from 1 to 64
- bond_atoms: int32 [2, 16, 64, 256], P(None, 'slab', 'dom'), may hold values from 0 to 511, as said below
- cross_atoms: int32 [2, 16, 64, 128], P(None, 'slab', 'dom'), may hold values from 0 to 255
- cross_side: int32 [16, 64, 128], P('slab', 'dom'), may hold values from 0 to 3
- cross_count: int32 [16, 64], P('slab', 'dom'), may hold values from 1 to 128
Outputs:
- coords_out: float32 [3, 16, 64, 512], P(None, 'slab', 'dom')
- velocity_out: float32 [3, 16, 64, 512], P(None, 'slab', 'dom')
The draws below stay inside these ranges and needn't reach their ends.
Inputs may be any that keep to these rules, and one draw needn't show every extreme that they name: `bond_atoms`: each bond joins two different atoms of the domain that holds it. `cross_atoms`: row 0 is an atom of the owning domain, row 1 an atom of the neighbour named by cross_side; both are among the first 256 atoms of their domains. `cross_side`: codes 0 to 3 name the in-slab neighbours at offsets +1, -1, +8, -8 along dom, cyclically. `cross_count`: slots below the count are live. `active_tile_count`: tiles below the count are live. `tile_atoms`: entries index the domain's halo list as in the first step.
All inputs are finite; a program needn't handle non-finite values.
Results may differ from the reference program's by a relative error of at most 0.0003.
Values sent between devices are 32-bit elements; how exact they have to be, the bound alone decides.
A program may use at most 32 MiB of HBM per device.

```python
import math
import jax
import jax.numpy as jnp
from jax import lax

ATOMS_DEV = 512
TILE = 128
ORDER = 4
CROSS_CAP = 128
SHELL = 256
TILES_DEV = 64
BONDS_DEV = 256
N_SLAB = 16
N_DOM = 64


def chain_order(device_key):
    return jax.random.permutation(device_key, ATOMS_DEV)


def draw_bond_atoms(key, part):
    device_keys = jax.random.split(jax.random.fold_in(key, 17), N_SLAB * N_DOM)
    orders = jax.vmap(chain_order)(device_keys).astype(jnp.int32)
    bond_left = orders[:, :BONDS_DEV]
    bond_partner_right = orders[:, 1:BONDS_DEV + 1]
    return jnp.stack([bond_left, bond_partner_right]).reshape(2, N_SLAB, N_DOM, BONDS_DEV)


def place_ends(values, key, low, high):
    shape = values.shape
    index_at = [jax.random.randint(jax.random.fold_in(key, axis), (), 0, shape[axis]) for axis in range(len(shape))]
    values = values.at[tuple(index_at)].set(low)
    longest = shape.index(max(shape))
    index_at[longest] = (index_at[longest] + 1) % shape[longest]
    return values.at[tuple(index_at)].set(high)


def shard_levels(own_key, shape, cuts, low, top_value):
    level = 1.0
    for axis_at, shards_of in cuts:
        heights = jax.random.uniform(jax.random.fold_in(jax.random.fold_in(own_key, 6), axis_at), (shards_of,), jnp.float32, low / len(cuts), top_value / len(cuts))
        level = level * jnp.repeat(jnp.exp(heights), shape[axis_at] // shards_of).reshape((-1,) + (1,) * (len(shape) - 1 - axis_at))
    return level


def bell_draw(stream_key, dims, deviation, limit, cuts=(), kind=jnp.bfloat16):
    result = jax.random.normal(stream_key, dims, jnp.float32) * deviation
    if len(cuts) > 0:
        result = shard_levels(stream_key, dims, cuts, -0.22, 0.18) * result
    return jnp.clip(result, min=-limit, max=limit).astype(kind)


def setup_inputs(seed: int = 0) -> dict:
    splits = jax.random.split(jax.random.key(seed), 12)
    return {
        "coords": bell_draw(splits[0], (3, N_SLAB, N_DOM, ATOMS_DEV), 1.0, 6.0, ((1, 16), (2, 64)), jnp.float32),
        "velocity": bell_draw(splits[1], (3, N_SLAB, N_DOM, ATOMS_DEV), 1.0, 6.0, ((1, 16), (2, 64)), jnp.float32),
        "charge": jnp.clip(jax.random.uniform(splits[2], (N_SLAB, N_DOM, ATOMS_DEV), jnp.float32, -1.0, 1.0) * shard_levels(splits[2], (N_SLAB, N_DOM, ATOMS_DEV), ((0, 16), (1, 64)), -0.4, 0.0), -1.0, 1.0),
        "inv_mass": jnp.clip(jnp.exp(math.log(1.0) - 2.7725887 * jax.random.uniform(splits[3], (N_SLAB, N_DOM, ATOMS_DEV), jnp.float32) ** shard_levels(splits[3], (N_SLAB, N_DOM, ATOMS_DEV), ((0, 16), (1, 64)), -0.2, 0.2)), 0.0625, 1.0),
        "tile_block": place_ends(jax.random.randint(splits[4], (N_SLAB, N_DOM, TILES_DEV), 0, ATOMS_DEV // TILE), jax.random.fold_in(splits[4], 1), 0, (ATOMS_DEV // TILE) - 1).astype(jnp.int32),
        "tile_atoms": place_ends(jax.random.randint(splits[5], (N_SLAB, N_DOM, TILES_DEV, TILE), 0, ATOMS_DEV + 6 * SHELL), jax.random.fold_in(splits[5], 1), 0, (ATOMS_DEV + 6 * SHELL) - 1).astype(jnp.int32),
        "active_tile_count": place_ends(jax.random.randint(splits[6], (N_SLAB, N_DOM), 1, TILES_DEV + 1), jax.random.fold_in(splits[6], 1), 1, TILES_DEV).astype(jnp.int32),
        "bond_atoms": draw_bond_atoms(jax.random.fold_in(splits[11], 71), 0),
        "cross_atoms": place_ends(jax.random.randint(splits[8], (2, N_SLAB, N_DOM, CROSS_CAP), 0, SHELL), jax.random.fold_in(splits[8], 1), 0, SHELL - 1).astype(jnp.int32),
        "cross_side": place_ends(jax.random.randint(splits[9], (N_SLAB, N_DOM, CROSS_CAP), 0, 4), jax.random.fold_in(splits[9], 1), 0, 3).astype(jnp.int32),
        "cross_count": place_ends(jax.random.randint(splits[10], (N_SLAB, N_DOM), 1, CROSS_CAP + 1), jax.random.fold_in(splits[10], 1), 1, CROSS_CAP).astype(jnp.int32),
    }


time_step = 0.1
cutoff_sq = 16.0
force_scale = 4.0
length_floor = 0.25

def tile_force(own_data, halo_data, block_index, atom_ids, tile_index, live_count):
    near_data = lax.dynamic_slice_in_dim(own_data, block_index * TILE, TILE, 1)
    far_data = jnp.take(halo_data, atom_ids, axis=1)
    offset_vec = near_data[:3, :, None] - far_data[:3, None, :]
    dist_sq = lax.optimization_barrier(jnp.sum(offset_vec * offset_vec, axis=0))
    inverse = 1.0 / (dist_sq + 1.0)
    switch = jnp.maximum(1.0 - dist_sq / cutoff_sq, 0.0) ** 2
    strength = force_scale * (2.0 * inverse ** 3 - near_data[3][:, None] * far_data[3][None, :] * inverse ** 2) * switch
    forces = lax.optimization_barrier(jnp.sum(strength[None] * offset_vec, axis=2))
    return forces * (tile_index < live_count).astype(jnp.float32)

def block_sum(tile_wise_values, block_ids, atom_count):
    pick_entries = (block_ids[:, None] == jnp.arange(atom_count // TILE, dtype=jnp.int32)[None, :]).astype(jnp.float32)
    accumulated_sum = jnp.einsum('mz,max->azx', pick_entries, tile_wise_values, precision=lax.Precision.HIGHEST)
    return accumulated_sum.reshape(3, atom_count)

def geometry(atom_first, atom_second, mass_first, mass_second):
    offset_vec = atom_first - atom_second
    length = jnp.sqrt(lax.optimization_barrier(jnp.sum(offset_vec * offset_vec, axis=0)) + length_floor)
    return (offset_vec / length, lax.rsqrt(mass_first + mass_second))

def project_bond(direction, bond_scale, atom_first, atom_second):
    return bond_scale * lax.optimization_barrier(jnp.sum(direction * (atom_first - atom_second), axis=0))

def reference(coords, velocity, charge, inv_mass, tile_block, tile_atoms, active_tile_count, bond_atoms, cross_atoms, cross_side, cross_count):
    slab_count, domains, atom_count = (coords.shape[1], coords.shape[2], coords.shape[3])
    devices = slab_count * domains
    shell_size = atom_count // 2
    row_width = max(2, domains // 8)
    strides = (1, -1, row_width, -row_width)
    own_data = jnp.concatenate([coords, charge[None], inv_mass[None]], axis=0)
    outer_rim = own_data[..., :shell_size]
    pieces = [own_data] + [jnp.roll(outer_rim, -stride, axis=2) for stride in strides]
    pieces = pieces + [jnp.roll(outer_rim, 1, axis=1), jnp.roll(outer_rim, -1, axis=1)]
    halo_data = jnp.concatenate(pieces, axis=3)
    own_flat = jnp.moveaxis(own_data.reshape(5, devices, atom_count), 1, 0)
    halo_flat = jnp.moveaxis(halo_data.reshape(5, devices, -1), 1, 0)

    def device_forces(packed):
        own_one, halo_one, block_ids, atom_ids, live_count = packed
        tile_ids = jnp.arange(block_ids.shape[0], dtype=jnp.int32)
        tile_wise_values = jax.vmap(tile_force, in_axes=(None, None, 0, 0, 0, None))(own_one, halo_one, block_ids, atom_ids, tile_ids, live_count)
        return block_sum(tile_wise_values, block_ids, atom_count)
    forces = lax.map(device_forces, (own_flat, halo_flat, tile_block.reshape(devices, -1), tile_atoms.reshape(devices, -1, TILE), active_tile_count.reshape(devices)))
    forces = jnp.moveaxis(forces, 0, 1).reshape(3, slab_count, domains, atom_count)
    velocity_half = velocity + time_step * forces * inv_mass[None]
    displace = time_step * velocity_half
    updated_positions = coords + displace
    total_atoms = devices * atom_count
    flat_coords = coords.reshape(3, total_atoms)
    flattened_masses = inv_mass.reshape(total_atoms)
    flat_displace = displace.reshape(3, total_atoms)
    device_ids = jnp.arange(devices, dtype=jnp.int32)
    offset_base = (device_ids * atom_count)[:, None]
    bond_left = (bond_atoms[0].reshape(devices, -1) + offset_base).reshape(-1)
    bond_partner_right = (bond_atoms[1].reshape(devices, -1) + offset_base).reshape(-1)
    stride_table = jnp.array(strides, dtype=jnp.int32)
    side_code = cross_side.reshape(devices, -1)
    dom_index = (device_ids % domains)[:, None]
    layer_slab_number = (device_ids // domains)[:, None]
    other_device = layer_slab_number * domains + (dom_index + stride_table[side_code]) % domains
    cross_first = (cross_atoms[0].reshape(devices, -1) + offset_base).reshape(-1)
    cross_second = (other_device * atom_count + cross_atoms[1].reshape(devices, -1)).reshape(-1)
    slot_ids = jnp.arange(side_code.shape[1], dtype=jnp.int32)[None, :]
    cross_flag = (slot_ids < cross_count.reshape(devices, 1)).astype(jnp.float32).reshape(-1)
    atom_first = jnp.concatenate([bond_left, cross_first])
    atom_second = jnp.concatenate([bond_partner_right, cross_second])
    live_mask = jnp.concatenate([jnp.ones(bond_left.shape, jnp.float32), cross_flag])
    direction, bond_scale = geometry(flat_coords[:, atom_first], flat_coords[:, atom_second], flattened_masses[atom_first], flattened_masses[atom_second])
    residue = project_bond(direction, bond_scale, flat_displace[:, atom_first], flat_displace[:, atom_second]) * live_mask

    def collect(values):
        pushed = direction * (bond_scale * values)
        totals = jnp.zeros((3, total_atoms), jnp.float32).at[:, atom_first].add(pushed).at[:, atom_second].add(-pushed)
        return flattened_masses * totals
    accumulated_sum = residue
    for expansion in range(ORDER):
        spread_now = collect(residue)
        residue = residue - project_bond(direction, bond_scale, spread_now[:, atom_first], spread_now[:, atom_second]) * live_mask
        accumulated_sum = accumulated_sum + residue
    correction = collect(accumulated_sum).reshape(3, slab_count, domains, atom_count)
    return (updated_positions - correction, velocity_half - correction / time_step)
```

```python
import functools

import jax
import jax.numpy as jnp
from jax import lax
from jax.experimental import pallas as pl
from jax.experimental.pallas import tpu as pltpu
from jax.sharding import PartitionSpec as P

TILE = 128
ORDER = 4
GROUP = 8

time_step = 0.1
cutoff_sq = 16.0
force_scale = 4.0
length_floor = 0.25

MESH = pl.DeviceIdType.MESH
f32, bf16, i32 = jnp.float32, jnp.bfloat16, jnp.int32

MASS, NORM, ONE, CHARGE = 3, 4, 5, 6


def parts3(a):
    high = a.astype(bf16).astype(f32)
    rest = a - high
    mid = rest.astype(bf16).astype(f32)
    low = (rest - mid).astype(bf16).astype(f32)
    return high, mid, low


def lanes(table, index):
    return jnp.take_along_axis(table, index, axis=1, mode="promise_in_bounds")


def row_ids():
    return lax.broadcasted_iota(i32, (8, TILE), 0)


def packed(low, high):
    return jnp.where(row_ids() < 4, low, pltpu.roll(high, 4, 0))


def half(picked, group):
    return jnp.where((group & 1) == 1, pltpu.roll(picked, 4, 0), picked)


def from_packed(tables, index):
    low, group = index & (TILE - 1), index >> 7
    picked = lanes(tables[0], low)
    for k in range(1, len(tables)):
        picked = jnp.where((group >> 1) == k, lanes(tables[k], low), picked)
    return half(picked, group)


def spread_row(row):
    return jnp.broadcast_to(row, (8, TILE))


def direction(first, second, mask):
    offset = jnp.where(row_ids() < 3, first - second, 0.0)
    squared = jnp.sum(offset * offset, axis=0, keepdims=True)
    masses = (first + second)[MASS : MASS + 1, :]
    return offset * (lax.rsqrt(squared + length_floor) * lax.rsqrt(masses) * mask)


def project(scaled_dir, first, second):
    return jnp.sum(scaled_dir * (first - second), axis=0, keepdims=True)


def kernel(
    n_slab,
    n_dom,
    coords_ref,
    velocity_ref,
    charge_ref,
    mass_ref,
    block_ref,
    atoms_ref,
    live_ref,
    bond_ref,
    cross_ref,
    side_ref,
    cross_count_ref,
    coords_out_ref,
    velocity_out_ref,
    own_ref,
    speed_ref,
    halo_ref,
    slots_ref,
    their_slots_ref,
    near_ref,
    far_ref,
    far2_ref,
    bond_inc_ref,
    cross_inc_ref,
    field_ref,
    fields_in_ref,
    halo_send,
    halo_recv,
    slots_send,
    slots_recv,
    field_send,
    field_recv,
):
    slab, dom = lax.axis_index("slab"), lax.axis_index("dom")
    width = max(2, n_dom // 8)
    strides = (1, -1, width, -width)
    in_slab = [(slab, lax.rem(dom + n_dom - s, n_dom)) for s in strides]
    across = [(lax.rem(slab + n_slab + s, n_slab), dom) for s in (1, -1)]
    targets = in_slab + across

    barrier = pltpu.get_barrier_semaphore()
    for target in targets:
        pl.semaphore_signal(barrier, inc=1, device_id=target, device_id_type=MESH)

    x, y, z = (coords_ref[c, 0] for c in range(3))
    own_ref[0:1, :] = x
    own_ref[1:2, :] = y
    own_ref[2:3, :] = z
    own_ref[MASS : MASS + 1, :] = mass_ref[0]
    own_ref[NORM : NORM + 1, :] = x * x + y * y + z * z
    own_ref[ONE : ONE + 1, :] = jnp.ones_like(x)
    own_ref[CHARGE : CHARGE + 1, :] = charge_ref[0]
    own_ref[7:8, :] = jnp.zeros_like(x)
    slots_ref[...] = jnp.zeros_like(slots_ref)
    slots_ref[0:1, :] = cross_ref[0, 0]
    slots_ref[1:2, :] = cross_ref[1, 0]
    slot_ids = lax.broadcasted_iota(i32, (1, TILE), 1)
    slots_ref[2:3, :] = jnp.where(slot_ids < cross_count_ref[0, 0], side_ref[0], 8)

    pl.semaphore_wait(barrier, len(targets))
    copies = []
    halo_copies, slot_copies = [], []
    for n, target in enumerate(targets):
        halo_copies.append(
            pltpu.make_async_remote_copy(
                src_ref=own_ref.at[:, pl.ds(0, 2 * TILE)],
                dst_ref=halo_ref.at[n],
                send_sem=halo_send.at[n],
                recv_sem=halo_recv.at[n],
                device_id=target,
                device_id_type=MESH,
            )
        )
        halo_copies[-1].start()
    for n, target in enumerate(in_slab):
        slot_copies.append(
            pltpu.make_async_remote_copy(
                src_ref=slots_ref,
                dst_ref=their_slots_ref.at[n],
                send_sem=slots_send.at[n],
                recv_sem=slots_recv.at[n],
                device_id=target,
                device_id_type=MESH,
            )
        )
        slot_copies[-1].start()
    copies += halo_copies + slot_copies

    own = own_ref[...]
    rows = lax.broadcasted_iota(i32, own.shape, 0)
    norm = own[NORM : NORM + 1, :]
    distance = jnp.where(rows < 3, -2.0 * own, 0.0)
    distance = jnp.where(rows == NORM, 1.0, distance)
    distance = jnp.where(rows == ONE, norm + 1.0, distance)
    charges = jnp.where(rows == CHARGE, force_scale * own, 0.0)
    for half_at, table in enumerate((distance, charges)):
        h, m, l = parts3(table)
        near = jnp.transpose(jnp.concatenate([h, m, l, h, m, h], axis=0)).astype(bf16)
        for b in range(4):
            near_ref[b, half_at * TILE : (half_at + 1) * TILE, :] = near[
                b * TILE : (b + 1) * TILE, :
            ]

    own_packed = [packed(own[:, 2 * k * TILE : (2 * k + 1) * TILE], own[:, (2 * k + 1) * TILE : (2 * k + 2) * TILE]) for k in range(2)]
    ones = jnp.ones((1, TILE), f32)
    bond_ends, bond_dir = [], []
    atom_ids = lax.broadcasted_iota(i32, (TILE, 4 * TILE), 1).astype(f32)
    for g in range(2):
        ends = [spread_row(bond_ref[e, 0][:, g * TILE : (g + 1) * TILE]) for e in range(2)]
        bond_ends.append(ends)
        bond_dir.append(direction(*[from_packed(own_packed, e) for e in ends], ones))
        columns = [jnp.transpose(e.astype(f32))[:, 0:1] for e in ends]
        marks = [jnp.where(c == atom_ids, 1.0, 0.0) for c in columns]
        bond_inc_ref[g * TILE : (g + 1) * TILE, :] = (marks[0] - marks[1]).astype(bf16)

    for copy in slot_copies:
        copy.wait_recv()
    tables = [slots_ref[...]] + [their_slots_ref[n] for n in range(4)]
    cross_own, cross_far, masks = [], [], []
    sides = spread_row(tables[0][2:3, :])
    for n, table in enumerate(tables):
        mine, theirs = (0, 1) if n == 0 else (1, 0)
        cross_own.append(spread_row(table[mine : mine + 1, :]))
        cross_far.append(spread_row(table[theirs : theirs + 1, :]))
        code = table[2:3, :]
        alive = code < 4 if n == 0 else code == ((n - 1) ^ 1)
        masks.append(jnp.where(alive, 1.0, 0.0))
        column = jnp.transpose(cross_own[-1].astype(f32))[:, 0:1]
        cross_inc_ref[n * TILE : (n + 1) * TILE, :] = jnp.where(
            column == atom_ids[:, : 2 * TILE], 1.0, 0.0
        ).astype(bf16)

    for copy in halo_copies:
        copy.wait_recv()

    def far_ends(tables):
        low, group = cross_far[0] & (TILE - 1), cross_far[0] >> 7
        picked = lanes(tables[0], low)
        for k in range(1, 4):
            picked = jnp.where(sides == k, lanes(tables[k], low), picked)
        return [half(picked, group)] + [from_packed([tables[n]], cross_far[n + 1]) for n in range(4)]

    far_packed = [packed(halo_ref[n, :, 0:TILE], halo_ref[n, :, TILE : 2 * TILE]) for n in range(4)]
    near_ends = [from_packed(own_packed[:1], c) for c in cross_own]
    cross_dir = [direction(a, b, m) for a, b, m in zip(near_ends, far_ends(far_packed), masks)]

    def gather(group, carry):
        index = atoms_ref[0, 0, pl.ds(pl.multiple_of(group * GROUP, GROUP), GROUP), :]
        tables = [own_ref[:, g * TILE : (g + 1) * TILE] for g in range(4)]
        tables += [halo_ref[n, :, g * TILE : (g + 1) * TILE] for n in range(6) for g in range(2)]
        for r in range(GROUP):
            entry = spread_row(index[r : r + 1, :])
            low = entry & (TILE - 1)
            found = [lanes(t, low) for t in tables]
            for bit in range(4):
                upper = ((entry >> (7 + bit)) & 1) == 1
                found = [jnp.where(upper, b, a) for a, b in zip(found[::2], found[1::2])]
            h, m, l = parts3(found[0])
            far_ref[group * GROUP + r] = jnp.concatenate([h, h, h, m, m, l], axis=0).astype(bf16)
            far2_ref[group * GROUP + r] = jnp.concatenate([h, m], axis=0).astype(bf16)
        return carry

    n_tiles = atoms_ref.shape[2]
    lax.fori_loop(0, n_tiles // GROUP, gather, 0)

    def pairs(group, totals):
        for r in range(GROUP):
            tile = group * GROUP + r
            block = block_ref[0, 0, tile]
            both = jnp.dot(near_ref[block], far_ref[tile], preferred_element_type=f32)
            dist, charge = both[:TILE], both[TILE:]
            inverse = 1.0 / dist
            switch = jnp.maximum((1.0 + 1.0 / cutoff_sq) - dist * (1.0 / cutoff_sq), 0.0)
            strength = (2.0 * force_scale * inverse - charge) * ((inverse * switch) * (inverse * switch))
            high = strength.astype(bf16)
            rest = (strength - high.astype(f32)).astype(bf16)
            summed = lax.dot_general(
                far2_ref[tile],
                jnp.concatenate([high, rest], axis=0),
                (((1,), (1,)), ((), ())),
                preferred_element_type=f32,
            )
            summed = summed[:, :TILE] + summed[:, TILE:]
            summed = summed[:8] + summed[8:]
            alive = jnp.where(tile < live_ref[0, 0], 1, 0)
            totals = tuple(
                t + summed * jnp.where(block == b, alive, 0).astype(f32)
                for b, t in enumerate(totals)
            )
        return totals

    totals = lax.fori_loop(
        0, n_tiles // GROUP, pairs, tuple(jnp.zeros((8, TILE), f32) for _ in range(4))
    )
    totals = jnp.concatenate(totals, axis=1)
    speed_ref[...] = jnp.zeros_like(speed_ref)
    for c in range(3):
        speed_ref[c : c + 1, :] = velocity_ref[c, 0]
    mass = own[MASS : MASS + 1, :]
    force = jnp.where(rows < 3, own * totals[ONE : ONE + 1, :] - totals, 0.0)
    velocity_half = speed_ref[...] + time_step * force * mass
    displace = time_step * velocity_half

    def exchange(step, shell):
        field_ref[step] = shell
        sent = []
        for n, target in enumerate(in_slab):
            sent.append(
                pltpu.make_async_remote_copy(
                    src_ref=field_ref.at[step],
                    dst_ref=fields_in_ref.at[step, n],
                    send_sem=field_send.at[step, n],
                    recv_sem=field_recv.at[step, n],
                    device_id=target,
                    device_id_type=MESH,
                )
            )
            sent[-1].start()
        return sent

    def changes(step, field):
        parts = [field[:, g * TILE : (g + 1) * TILE] for g in range(4)]
        tables = [packed(parts[0], parts[1]), packed(parts[2], parts[3])]
        sent = exchange(step, tables[0])
        copies.extend(sent)
        local = [project(d, from_packed(tables, a), from_packed(tables, b)) for d, (a, b) in zip(bond_dir, bond_ends)]
        here = [from_packed(tables[:1], c) for c in cross_own]
        for copy in sent:
            copy.wait_recv()
        there = far_ends([fields_in_ref[step, n] for n in range(4)])
        return local + [project(d, a, b) for d, a, b in zip(cross_dir, here, there)]

    scaled_dirs = bond_dir + cross_dir

    def spread(values):
        pushed = jnp.concatenate([d * v for d, v in zip(scaled_dirs, values)], axis=1)
        high = pushed.astype(bf16).astype(f32)
        pushed = jnp.concatenate([high, pushed - high], axis=0).astype(bf16)
        bonds = jnp.dot(pushed[:, : 2 * TILE], bond_inc_ref[...], preferred_element_type=f32)
        cross = jnp.dot(pushed[:, 2 * TILE :], cross_inc_ref[...], preferred_element_type=f32)
        total = jnp.concatenate([bonds[:, : 2 * TILE] + cross, bonds[:, 2 * TILE :]], axis=1)
        return (total[:8] + total[8:]) * mass

    residue = changes(0, displace)
    summed = residue
    for step in range(1, ORDER + 1):
        residue = [r - c for r, c in zip(residue, changes(step, spread(residue)))]
        summed = [s + r for s, r in zip(summed, residue)]
    correction = spread(summed)
    coords_out = own + displace - correction
    velocity_out = velocity_half - correction * (1.0 / time_step)
    for c in range(3):
        coords_out_ref[c, 0] = coords_out[c : c + 1, :]
        velocity_out_ref[c, 0] = velocity_out[c : c + 1, :]
    for copy in copies:
        copy.wait_send()


def shards(coords, velocity, charge, inv_mass, tile_block, tile_atoms, active_tile_count, bond_atoms, cross_atoms, cross_side, cross_count):
    n_slab, n_dom = lax.axis_size("slab"), lax.axis_size("dom")
    atoms = coords.shape[-1]
    tiles = tile_atoms.shape[2]
    vmem, smem = pl.BlockSpec(memory_space=pltpu.VMEM), pl.BlockSpec(memory_space=pltpu.SMEM)
    shape = jax.ShapeDtypeStruct(coords.shape, f32)
    return pl.pallas_call(
        functools.partial(kernel, n_slab, n_dom),
        out_shape=(shape, shape),
        in_specs=[vmem, vmem, vmem, vmem, smem, vmem, smem, vmem, vmem, vmem, smem],
        out_specs=(vmem, vmem),
        scratch_shapes=[
            pltpu.VMEM((8, atoms), f32),
            pltpu.VMEM((8, atoms), f32),
            pltpu.VMEM((6, 8, 2 * TILE), f32),
            pltpu.VMEM((8, TILE), i32),
            pltpu.VMEM((4, 8, TILE), i32),
            pltpu.VMEM((4, 2 * TILE, 48), bf16),
            pltpu.VMEM((tiles, 48, TILE), bf16),
            pltpu.VMEM((tiles, 16, TILE), bf16),
            pltpu.VMEM((2 * TILE, atoms), bf16),
            pltpu.VMEM((5 * TILE, 2 * TILE), bf16),
            pltpu.VMEM((ORDER + 1, 8, TILE), f32),
            pltpu.VMEM((ORDER + 1, 4, 8, TILE), f32),
            pltpu.SemaphoreType.DMA((6,)),
            pltpu.SemaphoreType.DMA((6,)),
            pltpu.SemaphoreType.DMA((4,)),
            pltpu.SemaphoreType.DMA((4,)),
            pltpu.SemaphoreType.DMA((ORDER + 1, 4)),
            pltpu.SemaphoreType.DMA((ORDER + 1, 4)),
        ],
        compiler_params=pltpu.CompilerParams(collective_id=0, has_side_effects=True),
    )(coords, velocity, charge, inv_mass, tile_block, tile_atoms, active_tile_count, bond_atoms, cross_atoms, cross_side, cross_count)


def solution(mesh):
    return jax.shard_map(
        shards,
        mesh=mesh,
        in_specs=(
            P(None, "slab", "dom", None),
            P(None, "slab", "dom", None),
            P("slab", "dom", None),
            P("slab", "dom", None),
            P("slab", "dom", None),
            P("slab", "dom", None, None),
            P("slab", "dom"),
            P(None, "slab", "dom", None),
            P(None, "slab", "dom", None),
            P("slab", "dom", None),
            P("slab", "dom"),
        ),
        out_specs=(P(None, "slab", "dom", None), P(None, "slab", "dom", None)),
        check_vma=False,
    )
```

```python
import functools

import jax
import jax.numpy as jnp
from jax import lax
from jax.experimental import pallas as pl
from jax.experimental.pallas import tpu as pltpu
from jax.sharding import PartitionSpec as P

TILE = 128
GROUP = 8

time_step = 0.1
cutoff_sq = 16.0
force_scale = 4.0
length_floor = 0.25

MESH = pl.DeviceIdType.MESH
f32, bf16, i32 = jnp.float32, jnp.bfloat16, jnp.int32

FOURTH = 3
DEPTH = 80
TWO_STEPS = ((0, 0), (1, 1), (2, 2), (3, 3), (0, 2), (0, 3), (1, 2), (1, 3))


def parts3(a):
    high = a.astype(bf16).astype(f32)
    rest = a - high
    mid = rest.astype(bf16).astype(f32)
    low = (rest - mid).astype(bf16).astype(f32)
    return high, mid, low


def lanes(table, index):
    return jnp.take_along_axis(table, index, axis=1, mode="promise_in_bounds")


def row_ids():
    return lax.broadcasted_iota(i32, (8, TILE), 0)


def packed(low, high):
    return jnp.where(row_ids() < 4, low, pltpu.roll(high, 4, 0))


def pack_field(field, halves=2):
    parts = [field[:, g * TILE : (g + 1) * TILE] for g in range(2 * halves)]
    return [packed(a, b) for a, b in zip(parts[::2], parts[1::2])]


def half(picked, group):
    return jnp.where((group & 1) == 1, pltpu.roll(picked, 4, 0), picked)


def from_packed(tables, index):
    low, group = index & (TILE - 1), index >> 7
    picked = lanes(tables[0], low)
    for k in range(1, len(tables)):
        picked = jnp.where((group >> 1) == k, lanes(tables[k], low), picked)
    return half(picked, group)


def spread_row(row):
    return jnp.broadcast_to(row, (8, TILE))


def direction(first, second, mask):
    offset = jnp.where(row_ids() < 3, first - second, 0.0)
    squared = jnp.sum(offset * offset, axis=0, keepdims=True)
    masses = (first + second)[FOURTH : FOURTH + 1, :]
    return offset * (lax.rsqrt(squared + length_floor) * lax.rsqrt(masses) * mask)


def project(scaled_dir, first, second):
    return jnp.sum(scaled_dir * (first - second), axis=0, keepdims=True)


def marks(index, atom_ids):
    return jnp.where(jnp.transpose(index.astype(f32))[:, 0:1] == atom_ids, 1.0, 0.0)


class Domain:
    def __init__(self, bonds, slots, far_slots, own_geo, far_geo, bond_inc, cross_inc):
        self.bond_inc, self.cross_inc = bond_inc, cross_inc
        atom_ids = lax.broadcasted_iota(i32, (TILE, bond_inc.shape[1]), 1).astype(f32)
        self.bond_ends = []
        for g in range(2):
            ends = [spread_row(bonds[2 * e + g : 2 * e + g + 1, :]) for e in range(2)]
            self.bond_ends.append(ends)
            bond_inc[g * TILE : (g + 1) * TILE, :] = (
                marks(ends[0], atom_ids) - marks(ends[1], atom_ids)
            ).astype(bf16)
        self.sides = spread_row(slots[2:3, :])
        self.cross_own, self.cross_far, masks = [], [], []
        for n, table in enumerate([slots] + far_slots):
            mine, theirs = (0, 1) if n == 0 else (1, 0)
            self.cross_own.append(spread_row(table[mine : mine + 1, :]))
            self.cross_far.append(spread_row(table[theirs : theirs + 1, :]))
            code = table[2:3, :]
            alive = code < 4 if n == 0 else code == ((n - 1) ^ 1)
            masks.append(jnp.where(alive, 1.0, 0.0))
            cross_inc[n * TILE : (n + 1) * TILE, :] = marks(
                self.cross_own[-1], atom_ids[:, : 2 * TILE]
            ).astype(bf16)
        ones = jnp.ones((1, TILE), f32)
        self.dirs = [
            direction(a, b, m)
            for (a, b), m in zip(
                self.bond_fields(own_geo) + self.cross_fields(own_geo, far_geo), [ones, ones] + masks
            )
        ]

    def bond_fields(self, own):
        return [(from_packed(own, a), from_packed(own, b)) for a, b in self.bond_ends]

    def cross_fields(self, own, far):
        here = [from_packed(own[:1], c) for c in self.cross_own]
        low, group = self.cross_far[0] & (TILE - 1), self.cross_far[0] >> 7
        picked = lanes(far[0], low)
        for k in range(1, 4):
            picked = jnp.where(self.sides == k, lanes(far[k], low), picked)
        there = [half(picked, group)] + [from_packed([far[k]], self.cross_far[k + 1]) for k in range(4)]
        return list(zip(here, there))

    def bond_changes(self, own):
        return [project(d, a, b) for d, (a, b) in zip(self.dirs[:2], self.bond_fields(own))]

    def cross_changes(self, own, far):
        return [project(d, a, b) for d, (a, b) in zip(self.dirs[2:], self.cross_fields(own, far))]

    def changes(self, own, far):
        return self.bond_changes(own) + self.cross_changes(own, far)

    def spread(self, values):
        pushed = jnp.concatenate([d * v for d, v in zip(self.dirs, values)], axis=1)
        high = pushed.astype(bf16).astype(f32)
        pushed = jnp.concatenate([high, pushed - high], axis=0).astype(bf16)
        bonds = jnp.dot(pushed[:, : 2 * TILE], self.bond_inc[...], preferred_element_type=f32)
        cross = jnp.dot(pushed[:, 2 * TILE :], self.cross_inc[...], preferred_element_type=f32)
        total = bonds[:, : 2 * TILE] + cross
        if bonds.shape[1] > 2 * TILE:
            total = jnp.concatenate([total, bonds[:, 2 * TILE :]], axis=1)
        return total[:8] + total[8:]


def kernel(
    n_slab,
    n_dom,
    coords_hbm,
    velocity_hbm,
    charge_hbm,
    mass_hbm,
    block_hbm,
    atoms_hbm,
    live_hbm,
    bond_hbm,
    cross_hbm,
    side_hbm,
    cross_count_hbm,
    moved_ref,
    velocity_half_ref,
    correction_ref,
    coords_ref,
    velocity_ref,
    charge_ref,
    mass_ref,
    block_ref,
    atoms_ref,
    live_ref,
    bond_ref,
    cross_ref,
    side_ref,
    cross_count_ref,
    load_sem,
    own_ref,
    speed_ref,
    rim_ref,
    inner_ref,
    rims_ref,
    index_ref,
    indices_ref,
    geo2_ref,
    slots2_ref,
    near_ref,
    bond_inc_ref,
    ghost_bond_inc_ref,
    cross_inc_ref,
    field_ref,
    fields_ref,
    fields2_ref,
    rim_send,
    rim_recv,
    index_send,
    index_recv,
    geo2_send,
    geo2_recv,
    slots2_send,
    slots2_recv,
    field_send,
    field_recv,
    field2_send,
    field2_recv,
):
    slab, dom = lax.axis_index("slab"), lax.axis_index("dom")
    width = max(2, n_dom // 8)
    strides = (1, -1, width, -width)

    def holder(stride):
        return slab, lax.rem(dom + 2 * n_dom - stride, n_dom)

    in_slab = [holder(s) for s in strides]
    across = [(lax.rem(slab + n_slab + s, n_slab), dom) for s in (1, -1)]
    beyond = [holder(strides[a] + strides[b]) for a, b in TWO_STEPS]
    targets = in_slab + across

    barrier = pltpu.get_barrier_semaphore()
    for target in targets:
        pl.semaphore_signal(barrier, inc=1, device_id=target, device_id_type=MESH)

    loads = [
        pltpu.make_async_copy(src, dst, load_sem.at[n])
        for n, (src, dst) in enumerate(
            (
                (coords_hbm, coords_ref),
                (charge_hbm, charge_ref),
                (mass_hbm, mass_ref),
                (cross_hbm, cross_ref),
                (side_hbm, side_ref),
                (cross_count_hbm, cross_count_ref),
                (bond_hbm, bond_ref),
                (velocity_hbm, velocity_ref),
                (block_hbm, block_ref),
                (live_hbm, live_ref),
                (atoms_hbm, atoms_ref),
            )
        )
    ]
    for load in loads:
        load.start()
    for load in loads[:7]:
        load.wait()

    for c in range(3):
        own_ref[c : c + 1, :] = coords_ref[c, 0]
        own_ref[4 + c : 5 + c, :] = coords_ref[c, 0]
    own_ref[3:4, :] = mass_ref[0]
    own_ref[7:8, :] = charge_ref[0]
    own = own_ref[...]
    rows = lax.broadcasted_iota(i32, own.shape, 0)
    parts = [own[:, g * TILE : (g + 1) * TILE] for g in range(4)]
    geo = [packed(parts[0], parts[1]), packed(parts[2], parts[3])]
    pair_tables = [jnp.where(row_ids() < 4, pltpu.roll(p, 4, 0), p) for p in parts]
    for g in range(2):
        rim_ref[g] = pair_tables[g]
        rim_ref[2 + g] = geo[g]
        inner_ref[g] = pair_tables[2 + g]
    index_ref[...] = jnp.zeros_like(index_ref)
    index_ref[0:1, :] = cross_ref[0, 0]
    index_ref[1:2, :] = cross_ref[1, 0]
    slot_ids = lax.broadcasted_iota(i32, (1, TILE), 1)
    index_ref[2:3, :] = jnp.where(slot_ids < cross_count_ref[0, 0], side_ref[0], 8)
    for e in range(2):
        for g in range(2):
            row = 8 + 2 * e + g
            index_ref[row : row + 1, :] = bond_ref[e, 0][:, g * TILE : (g + 1) * TILE]

    copies = []

    def send(src, dst, sent, landed, target):
        copy = pltpu.make_async_remote_copy(
            src_ref=src, dst_ref=dst, send_sem=sent, recv_sem=landed, device_id=target, device_id_type=MESH
        )
        copy.start()
        copies.append(copy)
        return copy

    pl.semaphore_wait(barrier, len(targets))
    rims = []
    for n, target in enumerate(targets):
        size = 4 if n < 4 else 2
        rims.append(send(rim_ref.at[pl.ds(0, size)], rims_ref.at[n, pl.ds(0, size)], rim_send.at[n], rim_recv.at[n], target))
    indices = [
        send(index_ref, indices_ref.at[n], index_send.at[n], index_recv.at[n], target)
        for n, target in enumerate(in_slab)
    ]

    norm = own[0:1, :] * own[0:1, :] + own[1:2, :] * own[1:2, :] + own[2:3, :] * own[2:3, :]
    zeros = jnp.zeros_like(own)
    distance = parts3(jnp.where(rows < 3, -2.0 * own, 0.0))
    charges = parts3(jnp.where(rows == 3, force_scale * pltpu.roll(own, 4, 0), 0.0))
    norms = parts3(norm + 1.0)
    for which in range(2):
        constant = jnp.where(rows == 4 * which, 1.0, 0.0)
        tails = [[jnp.where(rows == FOURTH, k, constant) for k in norms] + [zeros], [zeros] * 4]
        for at, ((h, m, l), tail) in enumerate(zip((distance, charges), tails)):
            pieces = [h, m, l, h, m, h]
            if which:
                pieces = [pltpu.roll(p, 4, 0) for p in pieces]
            near = jnp.transpose(jnp.concatenate(pieces + tail, axis=0)).astype(bf16)
            for b in range(4):
                near_ref[which, b, at * TILE : (at + 1) * TILE, :] = near[b * TILE : (b + 1) * TILE, :]

    for copy in indices:
        copy.wait_recv()
    for copy in rims:
        copy.wait_recv()
    geo2, slots2 = [], []
    for n, target in enumerate(beyond):
        geo2.append(send(rim_ref.at[2], geo2_ref.at[n], geo2_send.at[n], geo2_recv.at[n], target))
        slots2.append(send(index_ref.at[pl.ds(0, 8)], slots2_ref.at[n], slots2_send.at[n], slots2_recv.at[n], target))

    for load in loads[7:]:
        load.wait()

    def gather(group):
        index = atoms_ref[0, 0, pl.ds(pl.multiple_of(group * GROUP, GROUP), GROUP), :]
        fars = []
        tables = [rim_ref[0], rim_ref[1], inner_ref[0], inner_ref[1]]
        tables += [rims_ref[n, g] for n in range(6) for g in range(2)]
        ids = row_ids()
        for r in range(GROUP // 2):
            entry = jnp.where(ids < 4, spread_row(index[2 * r : 2 * r + 1, :]), spread_row(index[2 * r + 1 : 2 * r + 2, :]))
            low = entry & (TILE - 1)
            found = [lanes(t, low) for t in tables]
            for bit in range(4):
                upper = (entry & (TILE << bit)) != 0
                found = [jnp.where(upper, b, a) for a, b in zip(found[::2], found[1::2])]
            found = found[0]
            h, m, l = parts3(found)
            fourth = (ids & 3) == FOURTH
            square = jnp.where(fourth, 0.0, found * found)
            square = square + pltpu.roll(square, 7, 0) + pltpu.roll(square, 6, 0)
            squares = [jnp.where(ids == FOURTH, 1.0, s) for s in parts3(square)]
            far = jnp.concatenate([h, h, h, m, m, l] + squares + [jnp.zeros_like(h)], axis=0).astype(bf16)
            far2 = jnp.concatenate([jnp.where(fourth, 1.0, h), jnp.where(fourth, 0.0, m)], axis=0).astype(bf16)
            fars += [far, far2]
        return tuple(fars)

    n_groups = atoms_ref.shape[2] // GROUP

    def pairs(group, carry):
        totals, fars = list(carry[:8]), carry[8:]
        for r in range(GROUP // 2):
            far, far2 = fars[2 * r : 2 * r + 2]
            for which in range(2):
                tile = group * GROUP + 2 * r + which
                block = block_ref[0, 0, tile]
                both = jnp.dot(near_ref[which, block], far, preferred_element_type=f32)
                dist, charge = both[:TILE], both[TILE:]
                inverse = 1.0 / dist
                switch = jnp.maximum((1.0 + 1.0 / cutoff_sq) - dist * (1.0 / cutoff_sq), 0.0)
                edge = inverse * switch
                strength = (2.0 * force_scale * inverse - charge) * (edge * edge)
                high = strength.astype(bf16)
                rest = (strength - high.astype(f32)).astype(bf16)
                summed = lax.dot_general(
                    far2,
                    jnp.concatenate([high, rest], axis=0),
                    (((1,), (1,)), ((), ())),
                    preferred_element_type=f32,
                )
                summed = summed[:, :TILE] + summed[:, TILE:]
                summed = summed[:8] + summed[8:]
                alive = jnp.where(tile < live_ref[0, 0], 1, 0)
                for b in range(4):
                    weight = jnp.where(block == b, alive, 0).astype(f32)
                    totals[4 * which + b] = totals[4 * which + b] + summed * weight
        return tuple(totals) + gather(lax.rem(group + 1, n_groups))

    totals = lax.fori_loop(0, n_groups, pairs, tuple(jnp.zeros((8, TILE), f32) for _ in range(8)) + gather(0))[:8]
    totals = [packed_sum(a, b) for a, b in zip(totals[:4], totals[4:])]
    totals = jnp.concatenate(totals, axis=1)
    speed_ref[...] = jnp.zeros_like(speed_ref)
    for c in range(3):
        speed_ref[c : c + 1, :] = velocity_ref[c, 0]
    mass = own[3:4, :]
    force = jnp.where(rows < 3, own * totals[FOURTH : FOURTH + 1, :] - totals, 0.0)
    velocity_half = speed_ref[...] + time_step * force * mass
    displace = time_step * velocity_half
    moved = own + displace

    def exchange(step, tables):
        for g, table in enumerate(tables):
            field_ref[step, g] = table
        size = len(tables)
        sent = [
            send(
                field_ref.at[step, pl.ds(0, size)],
                fields_ref.at[step, n, pl.ds(0, size)],
                field_send.at[step, n],
                field_recv.at[step, n],
                target,
            )
            for n, target in enumerate(in_slab)
        ]
        if size == 2:
            sent += [
                send(field_ref.at[step, 0], fields2_ref.at[step, n], field2_send.at[step, n], field2_recv.at[step, n], target)
                for n, target in enumerate(beyond)
            ]
        return sent

    def arrive(sent):
        for copy in sent:
            copy.wait_recv()

    def around(n, mine, near_by, two_steps):
        found = []
        for k in range(4):
            pair = (n, k) if (n, k) in TWO_STEPS else (k, n)
            found.append(mine if k == n ^ 1 else two_steps[TWO_STEPS.index(pair)])
        return found

    displaced = pack_field(displace)
    sent = exchange(0, displaced)

    own_index = index_ref[...]
    near_index = [indices_ref[n] for n in range(4)]
    near_geo = [[rims_ref[n, 2], rims_ref[n, 3]] for n in range(4)]
    here = Domain(
        own_index[8:12, :],
        own_index[0:8, :],
        [i[0:8, :] for i in near_index],
        geo,
        [g[0] for g in near_geo],
        bond_inc_ref,
        cross_inc_ref.at[4],
    )
    arrive(geo2 + slots2)
    far_index = [slots2_ref[n] for n in range(8)]
    far_geo = [geo2_ref[n] for n in range(8)]
    ghosts, masses = [], []
    for n in range(4):
        ghosts.append(
            Domain(
                near_index[n][8:12, :],
                near_index[n][0:8, :],
                around(n, own_index[0:8, :], near_index, far_index),
                near_geo[n],
                around(n, geo[0], near_geo, far_geo),
                ghost_bond_inc_ref.at[n],
                cross_inc_ref.at[n],
            )
        )
        first = near_geo[n][0]
        masses.append(jnp.concatenate([first[FOURTH : FOURTH + 1, :], first[4 + FOURTH :, :]], axis=1))

    def ghost_changes(mine, step):
        by = [[fields_ref[step, n, g] for g in range(2)] for n in range(4)]
        two = [fields2_ref[step, n] for n in range(8)]
        return [ghosts[n].changes(by[n], around(n, mine[0], by, two)) for n in range(4)]

    def minus(a, b):
        return [x - y for x, y in zip(a, b)]

    def far_spread(values):
        return [pack_field(g.spread(v) * m, 1)[0] for g, v, m in zip(ghosts, values, masses)]

    local = here.bond_changes(displaced)
    arrive(sent)
    start = local + here.cross_changes(displaced, [fields_ref[0, n, 0] for n in range(4)])
    ghost_start = ghost_changes(displaced, 0)
    field1 = here.spread(start) * mass
    far = far_spread(ghost_start)
    first = minus(start, here.changes(pack_field(field1), far))
    field2 = field1 + here.spread(first) * mass
    both = pack_field(field2)
    sent = exchange(1, both)
    local = here.bond_changes(both)
    arrive(sent)
    second = minus(start, local + here.cross_changes(both, [fields_ref[1, n, 0] for n in range(4)]))
    ghost_second = [minus(a, b) for a, b in zip(ghost_start, ghost_changes(both, 1))]
    field3 = here.spread(second) * mass
    third = minus(second, here.changes(pack_field(field3), far_spread(ghost_second)))
    field4 = pack_field(here.spread(third) * mass)
    sent = exchange(2, field4[:1])
    local = here.bond_changes(field4)
    before = [a + b + c + 2.0 * d for a, b, c, d in zip(start, first, second, third)]
    arrive(sent)
    last = local + here.cross_changes(field4, [fields_ref[2, n, 0] for n in range(4)])
    correction = here.spread(minus(before, last)) * mass
    for c in range(3):
        moved_ref[c, 0] = moved[c : c + 1, :]
        velocity_half_ref[c, 0] = velocity_half[c : c + 1, :]
        correction_ref[c, 0] = correction[c : c + 1, :]
    for copy in copies:
        copy.wait_send()


def packed_sum(first, second):
    return first + pltpu.roll(second, 4, 0)


def shards(coords, velocity, charge, inv_mass, tile_block, tile_atoms, active_tile_count, bond_atoms, cross_atoms, cross_side, cross_count):
    n_slab, n_dom = lax.axis_size("slab"), lax.axis_size("dom")
    atoms = coords.shape[-1]
    tiles = tile_atoms.shape[2]
    shape = jax.ShapeDtypeStruct(coords.shape, f32)
    dma = pltpu.SemaphoreType.DMA
    moved, velocity_half, correction = pl.pallas_call(
        functools.partial(kernel, n_slab, n_dom),
        out_shape=(shape, shape, shape),
        in_specs=[pl.BlockSpec(memory_space=pl.ANY)] * 11,
        out_specs=(pl.BlockSpec(memory_space=pltpu.VMEM),) * 3,
        scratch_shapes=[
            pltpu.VMEM(coords.shape, f32),
            pltpu.VMEM(velocity.shape, f32),
            pltpu.VMEM(charge.shape, f32),
            pltpu.VMEM(inv_mass.shape, f32),
            pltpu.SMEM(tile_block.shape, i32),
            pltpu.VMEM(tile_atoms.shape, i32),
            pltpu.SMEM(active_tile_count.shape, i32),
            pltpu.VMEM(bond_atoms.shape, i32),
            pltpu.VMEM(cross_atoms.shape, i32),
            pltpu.VMEM(cross_side.shape, i32),
            pltpu.SMEM(cross_count.shape, i32),
            dma((11,)),
            pltpu.VMEM((8, atoms), f32),
            pltpu.VMEM((8, atoms), f32),
            pltpu.VMEM((4, 8, TILE), f32),
            pltpu.VMEM((2, 8, TILE), f32),
            pltpu.VMEM((6, 4, 8, TILE), f32),
            pltpu.VMEM((16, TILE), i32),
            pltpu.VMEM((4, 16, TILE), i32),
            pltpu.VMEM((8, 8, TILE), f32),
            pltpu.VMEM((8, 8, TILE), i32),
            pltpu.VMEM((2, 4, 2 * TILE, DEPTH), bf16),
            pltpu.VMEM((2 * TILE, atoms), bf16),
            pltpu.VMEM((4, 2 * TILE, 2 * TILE), bf16),
            pltpu.VMEM((5, 5 * TILE, 2 * TILE), bf16),
            pltpu.VMEM((3, 2, 8, TILE), f32),
            pltpu.VMEM((3, 4, 2, 8, TILE), f32),
            pltpu.VMEM((2, 8, 8, TILE), f32),
            dma((6,)),
            dma((6,)),
            dma((4,)),
            dma((4,)),
            dma((8,)),
            dma((8,)),
            dma((8,)),
            dma((8,)),
            dma((3, 4)),
            dma((3, 4)),
            dma((2, 8)),
            dma((2, 8)),
        ],
        compiler_params=pltpu.CompilerParams(collective_id=0, has_side_effects=True),
    )(coords, velocity, charge, inv_mass, tile_block, tile_atoms, active_tile_count, bond_atoms, cross_atoms, cross_side, cross_count)
    return moved - correction, velocity_half - correction / time_step


def solution(mesh):
    return jax.shard_map(
        shards,
        mesh=mesh,
        in_specs=(
            P(None, "slab", "dom", None),
            P(None, "slab", "dom", None),
            P("slab", "dom", None),
            P("slab", "dom", None),
            P("slab", "dom", None),
            P("slab", "dom", None, None),
            P("slab", "dom"),
            P(None, "slab", "dom", None),
            P(None, "slab", "dom", None),
            P("slab", "dom", None),
            P("slab", "dom"),
        ),
        out_specs=(P(None, "slab", "dom", None), P(None, "slab", "dom", None)),
        check_vma=False,
    )
```

```python
import functools

import jax
import jax.numpy as jnp
from jax import lax
from jax.experimental import pallas as pl
from jax.experimental.pallas import tpu as pltpu
from jax.sharding import PartitionSpec as P

TILE = 128
GROUP = 32

time_step = 0.1
cutoff_sq = 16.0
force_scale = 4.0
length_floor = 0.25

MESH = pl.DeviceIdType.MESH
f32, bf16, i32 = jnp.float32, jnp.bfloat16, jnp.int32

FOURTH = 3
DEPTH = 80
TWO_STEPS = ((0, 0), (1, 1), (2, 2), (3, 3), (0, 2), (0, 3), (1, 2), (1, 3))


def parts3(a):
    high = a.astype(bf16).astype(f32)
    rest = a - high
    mid = rest.astype(bf16).astype(f32)
    low = (rest - mid).astype(bf16).astype(f32)
    return high, mid, low


def lanes(table, index):
    return jnp.take_along_axis(table, index, axis=1, mode="promise_in_bounds")


def row_ids():
    return lax.broadcasted_iota(i32, (8, TILE), 0)


def packed(low, high):
    return jnp.where(row_ids() < 4, low, pltpu.roll(high, 4, 0))


def pack_field(field, halves=2):
    parts = [field[:, g * TILE : (g + 1) * TILE] for g in range(2 * halves)]
    return [packed(a, b) for a, b in zip(parts[::2], parts[1::2])]


def half(picked, group):
    return jnp.where((group & 1) == 1, pltpu.roll(picked, 4, 0), picked)


def from_packed(tables, index):
    low, group = index & (TILE - 1), index >> 7
    picked = lanes(tables[0], low)
    for k in range(1, len(tables)):
        picked = jnp.where((group >> 1) == k, lanes(tables[k], low), picked)
    return half(picked, group)


def spread_row(row):
    return jnp.broadcast_to(row, (8, TILE))


def direction(first, second, mask):
    offset = jnp.where(row_ids() < 3, first - second, 0.0)
    squared = jnp.sum(offset * offset, axis=0, keepdims=True)
    masses = (first + second)[FOURTH : FOURTH + 1, :]
    return offset * (lax.rsqrt(squared + length_floor) * lax.rsqrt(masses) * mask)


def project(scaled_dir, first, second):
    return jnp.sum(scaled_dir * (first - second), axis=0, keepdims=True)


def marks(index, atom_ids):
    return jnp.where(jnp.transpose(index.astype(f32))[:, 0:1] == atom_ids, 1.0, 0.0)


class Domain:
    def __init__(self, bonds, slots, far_slots, own_geo, far_geo, bond_inc, cross_inc):
        self.bond_inc, self.cross_inc = bond_inc, cross_inc
        atom_ids = lax.broadcasted_iota(i32, (TILE, bond_inc.shape[1]), 1).astype(f32)
        self.bond_ends = []
        for g in range(2):
            ends = [spread_row(bonds[2 * e + g : 2 * e + g + 1, :]) for e in range(2)]
            self.bond_ends.append(ends)
            bond_inc[g * TILE : (g + 1) * TILE, :] = (
                marks(ends[0], atom_ids) - marks(ends[1], atom_ids)
            ).astype(bf16)
        self.sides = spread_row(slots[2:3, :])
        self.cross_own, self.cross_far, masks = [], [], []
        for n, table in enumerate([slots] + far_slots):
            mine, theirs = (0, 1) if n == 0 else (1, 0)
            self.cross_own.append(spread_row(table[mine : mine + 1, :]))
            self.cross_far.append(spread_row(table[theirs : theirs + 1, :]))
            code = table[2:3, :]
            alive = code < 4 if n == 0 else code == ((n - 1) ^ 1)
            masks.append(jnp.where(alive, 1.0, 0.0))
            cross_inc[n * TILE : (n + 1) * TILE, :] = marks(
                self.cross_own[-1], atom_ids[:, : 2 * TILE]
            ).astype(bf16)
        ones = jnp.ones((1, TILE), f32)
        self.dirs = [
            direction(a, b, m)
            for (a, b), m in zip(
                self.bond_fields(own_geo) + self.cross_fields(own_geo, far_geo), [ones, ones] + masks
            )
        ]

    def bond_fields(self, own):
        return [(from_packed(own, a), from_packed(own, b)) for a, b in self.bond_ends]

    def cross_fields(self, own, far):
        here = [from_packed(own[:1], c) for c in self.cross_own]
        low, group = self.cross_far[0] & (TILE - 1), self.cross_far[0] >> 7
        picked = lanes(far[0], low)
        for k in range(1, 4):
            picked = jnp.where(self.sides == k, lanes(far[k], low), picked)
        there = [half(picked, group)] + [from_packed([far[k]], self.cross_far[k + 1]) for k in range(4)]
        return list(zip(here, there))

    def bond_changes(self, own):
        return [project(d, a, b) for d, (a, b) in zip(self.dirs[:2], self.bond_fields(own))]

    def cross_changes(self, own, far):
        return [project(d, a, b) for d, (a, b) in zip(self.dirs[2:], self.cross_fields(own, far))]

    def changes(self, own, far):
        return self.bond_changes(own) + self.cross_changes(own, far)

    def spread(self, values):
        pushed = jnp.concatenate([d * v for d, v in zip(self.dirs, values)], axis=1)
        high = pushed.astype(bf16).astype(f32)
        pushed = jnp.concatenate([high, pushed - high], axis=0).astype(bf16)
        bonds = jnp.dot(pushed[:, : 2 * TILE], self.bond_inc[...], preferred_element_type=f32)
        cross = jnp.dot(pushed[:, 2 * TILE :], self.cross_inc[...], preferred_element_type=f32)
        total = bonds[:, : 2 * TILE] + cross
        if bonds.shape[1] > 2 * TILE:
            total = jnp.concatenate([total, bonds[:, 2 * TILE :]], axis=1)
        return total[:8] + total[8:]


def kernel(
    n_slab,
    n_dom,
    coords_hbm,
    velocity_hbm,
    charge_hbm,
    mass_hbm,
    block_hbm,
    atoms_hbm,
    live_ref,
    bond_hbm,
    cross_hbm,
    side_hbm,
    cross_count_ref,
    moved_ref,
    velocity_half_ref,
    correction_ref,
    coords_ref,
    velocity_ref,
    charge_ref,
    mass_ref,
    block_ref,
    atoms_ref,
    bond_ref,
    cross_ref,
    side_ref,
    load_sem,
    own_ref,
    speed_ref,
    rim_ref,
    inner_ref,
    rims_ref,
    index_ref,
    indices_ref,
    geo2_ref,
    slots2_ref,
    near_ref,
    bond_inc_ref,
    ghost_bond_inc_ref,
    cross_inc_ref,
    field_ref,
    fields_ref,
    fields2_ref,
    rim_send,
    rim_recv,
    index_send,
    index_recv,
    geo2_send,
    geo2_recv,
    slots2_send,
    slots2_recv,
    field_send,
    field_recv,
    field2_send,
    field2_recv,
):
    slab, dom = lax.axis_index("slab"), lax.axis_index("dom")
    width = max(2, n_dom // 8)
    strides = (1, -1, width, -width)

    def holder(stride):
        return slab, lax.rem(dom + 2 * n_dom - stride, n_dom)

    in_slab = [holder(s) for s in strides]
    across = [(lax.rem(slab + n_slab + s, n_slab), dom) for s in (1, -1)]
    beyond = [holder(strides[a] + strides[b]) for a, b in TWO_STEPS]
    targets = in_slab + across

    barrier = pltpu.get_barrier_semaphore()
    for target in targets:
        pl.semaphore_signal(barrier, inc=1, device_id=target, device_id_type=MESH)

    loads = [
        pltpu.make_async_copy(src, dst, load_sem.at[n])
        for n, (src, dst) in enumerate(
            (
                (coords_hbm, coords_ref),
                (charge_hbm, charge_ref),
                (mass_hbm, mass_ref),
                (cross_hbm, cross_ref),
                (side_hbm, side_ref),
                (bond_hbm, bond_ref),
                (velocity_hbm, velocity_ref),
                (block_hbm, block_ref),
                (atoms_hbm, atoms_ref),
            )
        )
    ]
    for load in loads:
        load.start()
    for load in loads[:6]:
        load.wait()

    for c in range(3):
        own_ref[c : c + 1, :] = coords_ref[c, 0]
        own_ref[4 + c : 5 + c, :] = coords_ref[c, 0]
    own_ref[3:4, :] = mass_ref[0]
    own_ref[7:8, :] = charge_ref[0]
    own = own_ref[...]
    rows = lax.broadcasted_iota(i32, own.shape, 0)
    parts = [own[:, g * TILE : (g + 1) * TILE] for g in range(4)]
    geo = [packed(parts[0], parts[1]), packed(parts[2], parts[3])]
    pair_tables = [jnp.where(row_ids() < 4, pltpu.roll(p, 4, 0), p) for p in parts]
    for g in range(2):
        rim_ref[g] = pair_tables[g]
        rim_ref[2 + g] = geo[g]
        inner_ref[g] = pair_tables[2 + g]
    index_ref[...] = jnp.zeros_like(index_ref)
    index_ref[0:1, :] = cross_ref[0, 0]
    index_ref[1:2, :] = cross_ref[1, 0]
    slot_ids = lax.broadcasted_iota(i32, (1, TILE), 1)
    index_ref[2:3, :] = jnp.where(slot_ids < cross_count_ref[...], side_ref[0], 8)
    for e in range(2):
        for g in range(2):
            row = 8 + 2 * e + g
            index_ref[row : row + 1, :] = bond_ref[e, 0][:, g * TILE : (g + 1) * TILE]

    copies = []

    def send(src, dst, sent, landed, target):
        copy = pltpu.make_async_remote_copy(
            src_ref=src, dst_ref=dst, send_sem=sent, recv_sem=landed, device_id=target, device_id_type=MESH
        )
        copy.start()
        copies.append(copy)
        return copy

    pl.semaphore_wait(barrier, len(targets))
    rims = []
    for n, target in enumerate(targets):
        size = 4 if n < 4 else 2
        rims.append(send(rim_ref.at[pl.ds(0, size)], rims_ref.at[n, pl.ds(0, size)], rim_send.at[n], rim_recv.at[n], target))
    indices = [
        send(index_ref, indices_ref.at[n], index_send.at[n], index_recv.at[n], target)
        for n, target in enumerate(in_slab)
    ]

    norm = own[0:1, :] * own[0:1, :] + own[1:2, :] * own[1:2, :] + own[2:3, :] * own[2:3, :]
    zeros = jnp.zeros_like(own)
    distance = parts3(jnp.where(rows < 3, (-2.0 / cutoff_sq) * own, 0.0))
    charges = parts3(jnp.where(rows == 3, 2.0 * force_scale * pltpu.roll(own, 4, 0), 0.0))
    norms = parts3((norm + 1.0) * (1.0 / cutoff_sq))
    for which in range(2):
        constant = jnp.where(rows == 4 * which, 1.0 / cutoff_sq, 0.0)
        tails = [[jnp.where(rows == FOURTH, k, constant) for k in norms] + [zeros], [zeros] * 4]
        for at, ((h, m, l), tail) in enumerate(zip((distance, charges), tails)):
            pieces = [h, m, l, h, m, h]
            if which:
                pieces = [pltpu.roll(p, 4, 0) for p in pieces]
            near = jnp.transpose(jnp.concatenate(pieces + tail, axis=0)).astype(bf16)
            for b in range(4):
                near_ref[which, b, at * TILE : (at + 1) * TILE, :] = near[b * TILE : (b + 1) * TILE, :]

    for copy in indices:
        copy.wait_recv()
    for copy in rims:
        copy.wait_recv()
    geo2, slots2 = [], []
    for n, target in enumerate(beyond):
        geo2.append(send(rim_ref.at[2], geo2_ref.at[n], geo2_send.at[n], geo2_recv.at[n], target))
        slots2.append(send(index_ref.at[pl.ds(0, 8)], slots2_ref.at[n], slots2_send.at[n], slots2_recv.at[n], target))

    for load in loads[6:]:
        load.wait()

    def gather(group):
        index = atoms_ref[0, 0, pl.ds(pl.multiple_of(group * GROUP, GROUP), GROUP), :]
        fars = []
        tables = [rim_ref[0], rim_ref[1], inner_ref[0], inner_ref[1]]
        tables += [rims_ref[n, g] for n in range(6) for g in range(2)]
        ids = row_ids()
        for r in range(GROUP // 2):
            entry = jnp.where(ids < 4, spread_row(index[2 * r : 2 * r + 1, :]), spread_row(index[2 * r + 1 : 2 * r + 2, :]))
            low = entry & (TILE - 1)
            found = [lanes(t, low) for t in tables]
            for bit in range(4):
                upper = (entry & (TILE << bit)) != 0
                found = [jnp.where(upper, b, a) for a, b in zip(found[::2], found[1::2])]
            found = found[0]
            h, m, l = parts3(found)
            fourth = (ids & 3) == FOURTH
            square = jnp.where(fourth, 0.0, found * found)
            square = square + pltpu.roll(square, 7, 0) + pltpu.roll(square, 6, 0)
            squares = [jnp.where(ids == FOURTH, 1.0, s) for s in parts3(square)]
            far = jnp.concatenate([h, h, h, m, m, l] + squares + [jnp.zeros_like(h)], axis=0).astype(bf16)
            far2 = jnp.concatenate([jnp.where(fourth, 1.0, h), jnp.where(fourth, 0.0, m)], axis=0).astype(bf16)
            fars += [far, far2]
        return tuple(fars)

    n_groups = atoms_ref.shape[2] // GROUP
    live = live_ref[...]

    def pairs(group, carry):
        totals, fars = list(carry[:8]), carry[8:]
        for r in range(GROUP // 2):
            far, far2 = fars[2 * r : 2 * r + 2]
            blocks = [block_ref[0, 0, group * GROUP + 2 * r + which] for which in range(2)]
            near = jnp.concatenate([near_ref[which, blocks[which]] for which in range(2)], axis=0)
            both = jnp.dot(near, far, preferred_element_type=f32)
            for which, block in enumerate(blocks):
                tile = group * GROUP + 2 * r + which
                dist, charge = (both[k * TILE : (k + 1) * TILE] for k in (2 * which, 2 * which + 1))
                inverse = 1.0 / dist
                edge = inverse * jnp.maximum((1.0 + 1.0 / cutoff_sq) - dist, 0.0)
                strength = (inverse - charge) * (edge * edge)
                high = strength.astype(bf16)
                rest = (strength - high.astype(f32)).astype(bf16)
                summed = lax.dot_general(
                    far2,
                    jnp.concatenate([high, rest], axis=0),
                    (((1,), (1,)), ((), ())),
                    preferred_element_type=f32,
                )
                summed = summed[:, :TILE] + summed[:, TILE:]
                summed = summed[:8] + summed[8:]
                summed = summed * jnp.where(tile < live, 1.0, 0.0)
                for b in range(4):
                    weight = jnp.where(block == b, 1, 0).astype(f32)
                    totals[4 * which + b] = totals[4 * which + b] + summed * weight
        return tuple(totals) + gather(lax.rem(group + 1, n_groups))

    totals = lax.fori_loop(0, n_groups, pairs, tuple(jnp.zeros((8, TILE), f32) for _ in range(8)) + gather(0))[:8]
    totals = [packed_sum(a, b) for a, b in zip(totals[:4], totals[4:])]
    totals = jnp.concatenate(totals, axis=1) * (1.0 / 512.0)
    speed_ref[...] = jnp.zeros_like(speed_ref)
    for c in range(3):
        speed_ref[c : c + 1, :] = velocity_ref[c, 0]
    mass = own[3:4, :]
    force = jnp.where(rows < 3, own * totals[FOURTH : FOURTH + 1, :] - totals, 0.0)
    velocity_half = speed_ref[...] + time_step * force * mass
    displace = time_step * velocity_half
    moved = own + displace

    def exchange(step, tables):
        for g, table in enumerate(tables):
            field_ref[step, g] = table
        size = len(tables)
        sent = [
            send(
                field_ref.at[step, pl.ds(0, size)],
                fields_ref.at[step, n, pl.ds(0, size)],
                field_send.at[step, n],
                field_recv.at[step, n],
                target,
            )
            for n, target in enumerate(in_slab)
        ]
        if size == 2:
            sent += [
                send(field_ref.at[step, 0], fields2_ref.at[step, n], field2_send.at[step, n], field2_recv.at[step, n], target)
                for n, target in enumerate(beyond)
            ]
        return sent

    def arrive(sent):
        for copy in sent:
            copy.wait_recv()

    def around(n, mine, near_by, two_steps):
        found = []
        for k in range(4):
            pair = (n, k) if (n, k) in TWO_STEPS else (k, n)
            found.append(mine if k == n ^ 1 else two_steps[TWO_STEPS.index(pair)])
        return found

    displaced = pack_field(displace)
    sent = exchange(0, displaced)

    own_index = index_ref[...]
    near_index = [indices_ref[n] for n in range(4)]
    near_geo = [[rims_ref[n, 2], rims_ref[n, 3]] for n in range(4)]
    here = Domain(
        own_index[8:12, :],
        own_index[0:8, :],
        [i[0:8, :] for i in near_index],
        geo,
        [g[0] for g in near_geo],
        bond_inc_ref,
        cross_inc_ref.at[4],
    )
    arrive(geo2 + slots2)
    far_index = [slots2_ref[n] for n in range(8)]
    far_geo = [geo2_ref[n] for n in range(8)]
    ghosts, masses = [], []
    for n in range(4):
        ghosts.append(
            Domain(
                near_index[n][8:12, :],
                near_index[n][0:8, :],
                around(n, own_index[0:8, :], near_index, far_index),
                near_geo[n],
                around(n, geo[0], near_geo, far_geo),
                ghost_bond_inc_ref.at[n],
                cross_inc_ref.at[n],
            )
        )
        first = near_geo[n][0]
        masses.append(jnp.concatenate([first[FOURTH : FOURTH + 1, :], first[4 + FOURTH :, :]], axis=1))

    def ghost_changes(mine, step):
        by = [[fields_ref[step, n, g] for g in range(2)] for n in range(4)]
        two = [fields2_ref[step, n] for n in range(8)]
        return [ghosts[n].changes(by[n], around(n, mine[0], by, two)) for n in range(4)]

    def minus(a, b):
        return [x - y for x, y in zip(a, b)]

    def far_spread(values):
        return [pack_field(g.spread(v) * m, 1)[0] for g, v, m in zip(ghosts, values, masses)]

    local = here.bond_changes(displaced)
    arrive(sent)
    start = local + here.cross_changes(displaced, [fields_ref[0, n, 0] for n in range(4)])
    ghost_start = ghost_changes(displaced, 0)
    field1 = here.spread(start) * mass
    far = far_spread(ghost_start)
    first = minus(start, here.changes(pack_field(field1), far))
    field2 = field1 + here.spread(first) * mass
    both = pack_field(field2)
    sent = exchange(1, both)
    local = here.bond_changes(both)
    arrive(sent)
    second = minus(start, local + here.cross_changes(both, [fields_ref[1, n, 0] for n in range(4)]))
    ghost_second = [minus(a, b) for a, b in zip(ghost_start, ghost_changes(both, 1))]
    field3 = here.spread(second) * mass
    third = minus(second, here.changes(pack_field(field3), far_spread(ghost_second)))
    field4 = pack_field(here.spread(third) * mass)
    sent = exchange(2, field4[:1])
    local = here.bond_changes(field4)
    before = [a + b + c + 2.0 * d for a, b, c, d in zip(start, first, second, third)]
    arrive(sent)
    last = local + here.cross_changes(field4, [fields_ref[2, n, 0] for n in range(4)])
    correction = here.spread(minus(before, last)) * mass
    for c in range(3):
        moved_ref[c, 0] = moved[c : c + 1, :]
        velocity_half_ref[c, 0] = velocity_half[c : c + 1, :]
        correction_ref[c, 0] = correction[c : c + 1, :]
    for copy in copies:
        copy.wait_send()


def packed_sum(first, second):
    return first + pltpu.roll(second, 4, 0)


def shards(coords, velocity, charge, inv_mass, tile_block, tile_atoms, active_tile_count, bond_atoms, cross_atoms, cross_side, cross_count):
    n_slab, n_dom = lax.axis_size("slab"), lax.axis_size("dom")
    atoms = coords.shape[-1]
    tiles = tile_atoms.shape[2]
    shape = jax.ShapeDtypeStruct(coords.shape, f32)
    dma = pltpu.SemaphoreType.DMA
    vmem = pl.BlockSpec(memory_space=pltpu.VMEM)
    moved, velocity_half, correction = pl.pallas_call(
        functools.partial(kernel, n_slab, n_dom),
        out_shape=(pltpu.VMEM(coords.shape, f32),) * 3,
        in_specs=[vmem if n in (6, 10) else pl.BlockSpec(memory_space=pl.ANY) for n in range(11)],
        out_specs=(pl.BlockSpec(memory_space=pltpu.VMEM),) * 3,
        scratch_shapes=[
            pltpu.VMEM(coords.shape, f32),
            pltpu.VMEM(velocity.shape, f32),
            pltpu.VMEM(charge.shape, f32),
            pltpu.VMEM(inv_mass.shape, f32),
            pltpu.SMEM(tile_block.shape, i32),
            pltpu.VMEM(tile_atoms.shape, i32),
            pltpu.VMEM(bond_atoms.shape, i32),
            pltpu.VMEM(cross_atoms.shape, i32),
            pltpu.VMEM(cross_side.shape, i32),
            dma((9,)),
            pltpu.VMEM((8, atoms), f32),
            pltpu.VMEM((8, atoms), f32),
            pltpu.VMEM((4, 8, TILE), f32),
            pltpu.VMEM((2, 8, TILE), f32),
            pltpu.VMEM((6, 4, 8, TILE), f32),
            pltpu.VMEM((16, TILE), i32),
            pltpu.VMEM((4, 16, TILE), i32),
            pltpu.VMEM((8, 8, TILE), f32),
            pltpu.VMEM((8, 8, TILE), i32),
            pltpu.VMEM((2, 4, 2 * TILE, DEPTH), bf16),
            pltpu.VMEM((2 * TILE, atoms), bf16),
            pltpu.VMEM((4, 2 * TILE, 2 * TILE), bf16),
            pltpu.VMEM((5, 5 * TILE, 2 * TILE), bf16),
            pltpu.VMEM((3, 2, 8, TILE), f32),
            pltpu.VMEM((3, 4, 2, 8, TILE), f32),
            pltpu.VMEM((2, 8, 8, TILE), f32),
            dma((6,)),
            dma((6,)),
            dma((4,)),
            dma((4,)),
            dma((8,)),
            dma((8,)),
            dma((8,)),
            dma((8,)),
            dma((3, 4)),
            dma((3, 4)),
            dma((2, 8)),
            dma((2, 8)),
        ],
        compiler_params=pltpu.CompilerParams(collective_id=0, has_side_effects=True),
    )(coords, velocity, charge, inv_mass, tile_block, tile_atoms, active_tile_count, bond_atoms, cross_atoms, cross_side, cross_count)
    return moved - correction, velocity_half - correction / time_step


def solution(mesh):
    return jax.shard_map(
        shards,
        mesh=mesh,
        in_specs=(
            P(None, "slab", "dom", None),
            P(None, "slab", "dom", None),
            P("slab", "dom", None),
            P("slab", "dom", None),
            P("slab", "dom", None),
            P("slab", "dom", None, None),
            P("slab", "dom"),
            P(None, "slab", "dom", None),
            P(None, "slab", "dom", None),
            P("slab", "dom", None),
            P("slab", "dom"),
        ),
        out_specs=(P(None, "slab", "dom", None), P(None, "slab", "dom", None)),
        check_vma=False,
    )
```

```python
import functools

import jax
import jax.numpy as jnp
from jax import lax
from jax.experimental import pallas as pl
from jax.experimental.pallas import tpu as pltpu
from jax.sharding import PartitionSpec as P

TILE = 128

time_step = 0.1
cutoff_sq = 16.0
force_scale = 4.0
length_floor = 0.25

MESH = pl.DeviceIdType.MESH
f32, bf16, i32 = jnp.float32, jnp.bfloat16, jnp.int32

FOURTH = 3
DEPTH = 80
TWO_STEPS = ((0, 0), (1, 1), (2, 2), (3, 3), (0, 2), (0, 3), (1, 2), (1, 3))


def parts3(a):
    high = a.astype(bf16).astype(f32)
    rest = a - high
    mid = rest.astype(bf16).astype(f32)
    low = (rest - mid).astype(bf16).astype(f32)
    return high, mid, low


def lanes(table, index):
    return jnp.take_along_axis(table, index, axis=1, mode="promise_in_bounds")


def row_ids():
    return lax.broadcasted_iota(i32, (8, TILE), 0)


def packed(low, high):
    return jnp.where(row_ids() < 4, low, pltpu.roll(high, 4, 0))


def pack_field(field, halves=2):
    parts = [field[:, g * TILE : (g + 1) * TILE] for g in range(2 * halves)]
    return [packed(a, b) for a, b in zip(parts[::2], parts[1::2])]


def half(picked, group):
    return jnp.where((group & 1) == 1, pltpu.roll(picked, 4, 0), picked)


def from_packed(tables, index):
    low, group = index & (TILE - 1), index >> 7
    picked = lanes(tables[0], low)
    for k in range(1, len(tables)):
        picked = jnp.where((group >> 1) == k, lanes(tables[k], low), picked)
    return half(picked, group)


def spread_row(row):
    return jnp.broadcast_to(row, (8, TILE))


def direction(first, second, mask):
    offset = jnp.where(row_ids() < 3, first - second, 0.0)
    squared = jnp.sum(offset * offset, axis=0, keepdims=True)
    masses = (first + second)[FOURTH : FOURTH + 1, :]
    return offset * (lax.rsqrt(squared + length_floor) * lax.rsqrt(masses) * mask)


def project(scaled_dir, first, second):
    return jnp.sum(scaled_dir * (first - second), axis=0, keepdims=True)


def marks(index, atom_ids):
    return jnp.where(jnp.transpose(index.astype(f32))[:, 0:1] == atom_ids, 1.0, 0.0)


class Domain:
    def __init__(self, bonds, slots, far_slots, own_geo, far_geo, bond_inc, cross_inc):
        self.bond_inc, self.cross_inc = bond_inc, cross_inc
        atom_ids = lax.broadcasted_iota(i32, (TILE, bond_inc.shape[1]), 1).astype(f32)
        self.bond_ends = []
        for g in range(2):
            ends = [spread_row(bonds[2 * e + g : 2 * e + g + 1, :]) for e in range(2)]
            self.bond_ends.append(ends)
            bond_inc[g * TILE : (g + 1) * TILE, :] = (
                marks(ends[0], atom_ids) - marks(ends[1], atom_ids)
            ).astype(bf16)
        self.sides = spread_row(slots[2:3, :])
        self.cross_own, self.cross_far, masks = [], [], []
        for n, table in enumerate([slots] + far_slots):
            mine, theirs = (0, 1) if n == 0 else (1, 0)
            self.cross_own.append(spread_row(table[mine : mine + 1, :]))
            self.cross_far.append(spread_row(table[theirs : theirs + 1, :]))
            code = table[2:3, :]
            alive = code < 4 if n == 0 else code == ((n - 1) ^ 1)
            masks.append(jnp.where(alive, 1.0, 0.0))
            cross_inc[n * TILE : (n + 1) * TILE, :] = marks(
                self.cross_own[-1], atom_ids[:, : 2 * TILE]
            ).astype(bf16)
        ones = jnp.ones((1, TILE), f32)
        self.dirs = [
            direction(a, b, m)
            for (a, b), m in zip(
                self.bond_fields(own_geo) + self.cross_fields(own_geo, far_geo), [ones, ones] + masks
            )
        ]

    def bond_fields(self, own):
        return [(from_packed(own, a), from_packed(own, b)) for a, b in self.bond_ends]

    def cross_fields(self, own, far):
        here = [from_packed(own[:1], c) for c in self.cross_own]
        low, group = self.cross_far[0] & (TILE - 1), self.cross_far[0] >> 7
        picked = lanes(far[0], low)
        for k in range(1, 4):
            picked = jnp.where(self.sides == k, lanes(far[k], low), picked)
        there = [half(picked, group)] + [from_packed([far[k]], self.cross_far[k + 1]) for k in range(4)]
        return list(zip(here, there))

    def bond_changes(self, own):
        return [project(d, a, b) for d, (a, b) in zip(self.dirs[:2], self.bond_fields(own))]

    def cross_changes(self, own, far):
        return [project(d, a, b) for d, (a, b) in zip(self.dirs[2:], self.cross_fields(own, far))]

    def changes(self, own, far):
        return self.bond_changes(own) + self.cross_changes(own, far)

    def spread(self, values):
        pushed = jnp.concatenate([d * v for d, v in zip(self.dirs, values)], axis=1)
        high = pushed.astype(bf16).astype(f32)
        pushed = jnp.concatenate([high, pushed - high], axis=0).astype(bf16)
        bonds = jnp.dot(pushed[:, : 2 * TILE], self.bond_inc[...], preferred_element_type=f32)
        cross = jnp.dot(pushed[:, 2 * TILE :], self.cross_inc[...], preferred_element_type=f32)
        total = bonds[:, : 2 * TILE] + cross
        if bonds.shape[1] > 2 * TILE:
            total = jnp.concatenate([total, bonds[:, 2 * TILE :]], axis=1)
        return total[:8] + total[8:]


def kernel(
    n_slab,
    n_dom,
    coords_hbm,
    velocity_hbm,
    charge_hbm,
    mass_hbm,
    block_hbm,
    atoms_hbm,
    live_ref,
    bond_hbm,
    cross_hbm,
    side_hbm,
    cross_count_ref,
    moved_ref,
    velocity_half_ref,
    correction_ref,
    coords_ref,
    velocity_ref,
    charge_ref,
    mass_ref,
    block_ref,
    atoms_ref,
    bond_ref,
    cross_ref,
    side_ref,
    load_sem,
    own_ref,
    speed_ref,
    rim_ref,
    inner_ref,
    rims_ref,
    index_ref,
    indices_ref,
    geo2_ref,
    slots2_ref,
    near_ref,
    bond_inc_ref,
    ghost_bond_inc_ref,
    cross_inc_ref,
    field_ref,
    fields_ref,
    fields2_ref,
    rim_send,
    rim_recv,
    index_send,
    index_recv,
    geo2_send,
    geo2_recv,
    slots2_send,
    slots2_recv,
    field_send,
    field_recv,
    field2_send,
    field2_recv,
):
    slab, dom = lax.axis_index("slab"), lax.axis_index("dom")
    width = max(2, n_dom // 8)
    strides = (1, -1, width, -width)

    def holder(stride):
        return slab, lax.rem(dom + 2 * n_dom - stride, n_dom)

    in_slab = [holder(s) for s in strides]
    across = [(lax.rem(slab + n_slab + s, n_slab), dom) for s in (1, -1)]
    beyond = [holder(strides[a] + strides[b]) for a, b in TWO_STEPS]
    targets = in_slab + across

    barrier = pltpu.get_barrier_semaphore()
    for target in targets:
        pl.semaphore_signal(barrier, inc=1, device_id=target, device_id_type=MESH)

    loads = [
        pltpu.make_async_copy(src, dst, load_sem.at[n])
        for n, (src, dst) in enumerate(
            (
                (coords_hbm, coords_ref),
                (charge_hbm, charge_ref),
                (mass_hbm, mass_ref),
                (cross_hbm, cross_ref),
                (side_hbm, side_ref),
                (bond_hbm, bond_ref),
                (velocity_hbm, velocity_ref),
                (block_hbm, block_ref),
                (atoms_hbm, atoms_ref),
            )
        )
    ]
    for load in loads:
        load.start()
    for load in loads[:6]:
        load.wait()

    for c in range(3):
        own_ref[c : c + 1, :] = coords_ref[c, 0]
        own_ref[4 + c : 5 + c, :] = coords_ref[c, 0]
    own_ref[3:4, :] = mass_ref[0]
    own_ref[7:8, :] = charge_ref[0]
    own = own_ref[...]
    rows = lax.broadcasted_iota(i32, own.shape, 0)
    parts = [own[:, g * TILE : (g + 1) * TILE] for g in range(4)]
    geo = [packed(parts[0], parts[1]), packed(parts[2], parts[3])]
    pair_tables = [jnp.where(row_ids() < 4, pltpu.roll(p, 4, 0), p) for p in parts]
    for g in range(2):
        rim_ref[g] = pair_tables[g]
        rim_ref[2 + g] = geo[g]
        inner_ref[g] = pair_tables[2 + g]
    index_ref[...] = jnp.zeros_like(index_ref)
    index_ref[0:1, :] = cross_ref[0, 0]
    index_ref[1:2, :] = cross_ref[1, 0]
    slot_ids = lax.broadcasted_iota(i32, (1, TILE), 1)
    index_ref[2:3, :] = jnp.where(slot_ids < cross_count_ref[...], side_ref[0], 8)
    for e in range(2):
        for g in range(2):
            row = 8 + 2 * e + g
            index_ref[row : row + 1, :] = bond_ref[e, 0][:, g * TILE : (g + 1) * TILE]

    copies = []

    def send(src, dst, sent, landed, target):
        copy = pltpu.make_async_remote_copy(
            src_ref=src, dst_ref=dst, send_sem=sent, recv_sem=landed, device_id=target, device_id_type=MESH
        )
        copy.start()
        copies.append(copy)
        return copy

    pl.semaphore_wait(barrier, len(targets))
    rims = []
    for n, target in enumerate(targets):
        size = 4 if n < 4 else 2
        rims.append(send(rim_ref.at[pl.ds(0, size)], rims_ref.at[n, pl.ds(0, size)], rim_send.at[n], rim_recv.at[n], target))
    indices = [
        send(index_ref, indices_ref.at[n], index_send.at[n], index_recv.at[n], target)
        for n, target in enumerate(in_slab)
    ]

    norm = own[0:1, :] * own[0:1, :] + own[1:2, :] * own[1:2, :] + own[2:3, :] * own[2:3, :]
    zeros = jnp.zeros_like(own)
    distance = parts3(jnp.where(rows < 3, (-2.0 / cutoff_sq) * own, 0.0))
    charges = parts3(jnp.where(rows == 3, 2.0 * force_scale * pltpu.roll(own, 4, 0), 0.0))
    norms = parts3((norm + 1.0) * (1.0 / cutoff_sq))
    for which in range(2):
        constant = jnp.where(rows == 4 * which, 1.0 / cutoff_sq, 0.0)
        tails = [[jnp.where(rows == FOURTH, k, constant) for k in norms] + [zeros], [zeros] * 4]
        for at, ((h, m, l), tail) in enumerate(zip((distance, charges), tails)):
            pieces = [h, m, l, h, m, h]
            if which:
                pieces = [pltpu.roll(p, 4, 0) for p in pieces]
            near = jnp.transpose(jnp.concatenate(pieces + tail, axis=0)).astype(bf16)
            for b in range(4):
                near_ref[which, b, at * TILE : (at + 1) * TILE, :] = near[b * TILE : (b + 1) * TILE, :]

    for copy in indices:
        copy.wait_recv()
    for copy in rims:
        copy.wait_recv()
    geo2, slots2 = [], []
    for n, target in enumerate(beyond):
        geo2.append(send(rim_ref.at[2], geo2_ref.at[n], geo2_send.at[n], geo2_recv.at[n], target))
        slots2.append(send(index_ref.at[pl.ds(0, 8)], slots2_ref.at[n], slots2_send.at[n], slots2_recv.at[n], target))

    for load in loads[6:]:
        load.wait()

    n_tiles = atoms_ref.shape[2]

    def gather():
        index = atoms_ref[0, 0]
        fars = []
        tables = [rim_ref[0], rim_ref[1], inner_ref[0], inner_ref[1]]
        tables += [rims_ref[n, g] for n in range(6) for g in range(2)]
        ids = row_ids()
        for r in range(n_tiles // 2):
            entry = jnp.where(ids < 4, spread_row(index[2 * r : 2 * r + 1, :]), spread_row(index[2 * r + 1 : 2 * r + 2, :]))
            low = entry & (TILE - 1)
            found = [lanes(t, low) for t in tables]
            for bit in range(4):
                upper = (entry & (TILE << bit)) != 0
                found = [jnp.where(upper, b, a) for a, b in zip(found[::2], found[1::2])]
            found = found[0]
            h, m, l = parts3(found)
            fourth = (ids & 3) == FOURTH
            square = jnp.where(fourth, 0.0, found * found)
            square = square + pltpu.roll(square, 7, 0) + pltpu.roll(square, 6, 0)
            squares = [jnp.where(ids == FOURTH, 1.0, s) for s in parts3(square)]
            far = jnp.concatenate([h, h, h, m, m, l] + squares + [jnp.zeros_like(h)], axis=0).astype(bf16)
            far2 = jnp.concatenate([jnp.where(fourth, 1.0, h), jnp.where(fourth, 0.0, m)], axis=0).astype(bf16)
            fars += [far, far2]
        return tuple(fars)

    live = live_ref[...]

    def pairs(fars):
        totals = [jnp.zeros((8, TILE), f32) for _ in range(8)]
        for r in range(n_tiles // 2):
            far, far2 = fars[2 * r : 2 * r + 2]
            blocks = [block_ref[0, 0, 2 * r + which] for which in range(2)]
            near = jnp.concatenate([near_ref[which, blocks[which]] for which in range(2)], axis=0)
            both = jnp.dot(near, far, preferred_element_type=f32)
            for which, block in enumerate(blocks):
                tile = 2 * r + which
                dist, charge = (both[k * TILE : (k + 1) * TILE] for k in (2 * which, 2 * which + 1))
                inverse = 1.0 / dist
                edge = inverse * jnp.maximum((1.0 + 1.0 / cutoff_sq) - dist, 0.0)
                strength = (inverse - charge) * (edge * edge)
                high = strength.astype(bf16)
                rest = (strength - high.astype(f32)).astype(bf16)
                summed = lax.dot_general(
                    far2,
                    jnp.concatenate([high, rest], axis=0),
                    (((1,), (1,)), ((), ())),
                    preferred_element_type=f32,
                )
                summed = summed[:, :TILE] + summed[:, TILE:]
                summed = summed[:8] + summed[8:]
                summed = summed * jnp.where(tile < live, 1.0, 0.0)
                for b in range(4):
                    weight = jnp.where(block == b, 1, 0).astype(f32)
                    totals[4 * which + b] = totals[4 * which + b] + summed * weight
        return totals

    totals = pairs(gather())
    totals = [packed_sum(a, b) for a, b in zip(totals[:4], totals[4:])]
    totals = jnp.concatenate(totals, axis=1) * (1.0 / 512.0)
    speed_ref[...] = jnp.zeros_like(speed_ref)
    for c in range(3):
        speed_ref[c : c + 1, :] = velocity_ref[c, 0]
    mass = own[3:4, :]
    force = jnp.where(rows < 3, own * totals[FOURTH : FOURTH + 1, :] - totals, 0.0)
    velocity_half = speed_ref[...] + time_step * force * mass
    displace = time_step * velocity_half
    moved = own + displace

    def exchange(step, tables):
        for g, table in enumerate(tables):
            field_ref[step, g] = table
        size = len(tables)
        sent = [
            send(
                field_ref.at[step, pl.ds(0, size)],
                fields_ref.at[step, n, pl.ds(0, size)],
                field_send.at[step, n],
                field_recv.at[step, n],
                target,
            )
            for n, target in enumerate(in_slab)
        ]
        if size == 2:
            sent += [
                send(field_ref.at[step, 0], fields2_ref.at[step, n], field2_send.at[step, n], field2_recv.at[step, n], target)
                for n, target in enumerate(beyond)
            ]
        return sent

    def arrive(sent):
        for copy in sent:
            copy.wait_recv()

    def around(n, mine, near_by, two_steps):
        found = []
        for k in range(4):
            pair = (n, k) if (n, k) in TWO_STEPS else (k, n)
            found.append(mine if k == n ^ 1 else two_steps[TWO_STEPS.index(pair)])
        return found

    displaced = pack_field(displace)
    sent = exchange(0, displaced)

    own_index = index_ref[...]
    near_index = [indices_ref[n] for n in range(4)]
    near_geo = [[rims_ref[n, 2], rims_ref[n, 3]] for n in range(4)]
    here = Domain(
        own_index[8:12, :],
        own_index[0:8, :],
        [i[0:8, :] for i in near_index],
        geo,
        [g[0] for g in near_geo],
        bond_inc_ref,
        cross_inc_ref.at[4],
    )
    arrive(geo2 + slots2)
    far_index = [slots2_ref[n] for n in range(8)]
    far_geo = [geo2_ref[n] for n in range(8)]
    ghosts, masses = [], []
    for n in range(4):
        ghosts.append(
            Domain(
                near_index[n][8:12, :],
                near_index[n][0:8, :],
                around(n, own_index[0:8, :], near_index, far_index),
                near_geo[n],
                around(n, geo[0], near_geo, far_geo),
                ghost_bond_inc_ref.at[n],
                cross_inc_ref.at[n],
            )
        )
        first = near_geo[n][0]
        masses.append(jnp.concatenate([first[FOURTH : FOURTH + 1, :], first[4 + FOURTH :, :]], axis=1))

    def ghost_changes(mine, step):
        by = [[fields_ref[step, n, g] for g in range(2)] for n in range(4)]
        two = [fields2_ref[step, n] for n in range(8)]
        return [ghosts[n].changes(by[n], around(n, mine[0], by, two)) for n in range(4)]

    def minus(a, b):
        return [x - y for x, y in zip(a, b)]

    def far_spread(values):
        return [pack_field(g.spread(v) * m, 1)[0] for g, v, m in zip(ghosts, values, masses)]

    local = here.bond_changes(displaced)
    arrive(sent)
    start = local + here.cross_changes(displaced, [fields_ref[0, n, 0] for n in range(4)])
    ghost_start = ghost_changes(displaced, 0)
    field1 = here.spread(start) * mass
    far = far_spread(ghost_start)
    first = minus(start, here.changes(pack_field(field1), far))
    field2 = field1 + here.spread(first) * mass
    both = pack_field(field2)
    sent = exchange(1, both)
    local = here.bond_changes(both)
    arrive(sent)
    second = minus(start, local + here.cross_changes(both, [fields_ref[1, n, 0] for n in range(4)]))
    ghost_second = [minus(a, b) for a, b in zip(ghost_start, ghost_changes(both, 1))]
    field3 = here.spread(second) * mass
    third = minus(second, here.changes(pack_field(field3), far_spread(ghost_second)))
    field4 = pack_field(here.spread(third) * mass)
    sent = exchange(2, field4[:1])
    local = here.bond_changes(field4)
    before = [a + b + c + 2.0 * d for a, b, c, d in zip(start, first, second, third)]
    arrive(sent)
    last = local + here.cross_changes(field4, [fields_ref[2, n, 0] for n in range(4)])
    correction = here.spread(minus(before, last)) * mass
    for c in range(3):
        moved_ref[c, 0] = moved[c : c + 1, :]
        velocity_half_ref[c, 0] = velocity_half[c : c + 1, :]
        correction_ref[c, 0] = correction[c : c + 1, :]
    for copy in copies:
        copy.wait_send()


def packed_sum(first, second):
    return first + pltpu.roll(second, 4, 0)


def shards(coords, velocity, charge, inv_mass, tile_block, tile_atoms, active_tile_count, bond_atoms, cross_atoms, cross_side, cross_count):
    n_slab, n_dom = lax.axis_size("slab"), lax.axis_size("dom")
    atoms = coords.shape[-1]
    tiles = tile_atoms.shape[2]
    shape = jax.ShapeDtypeStruct(coords.shape, f32)
    dma = pltpu.SemaphoreType.DMA
    vmem = pl.BlockSpec(memory_space=pltpu.VMEM)
    moved, velocity_half, correction = pl.pallas_call(
        functools.partial(kernel, n_slab, n_dom),
        out_shape=(pltpu.VMEM(coords.shape, f32),) * 3,
        in_specs=[vmem if n in (6, 10) else pl.BlockSpec(memory_space=pl.ANY) for n in range(11)],
        out_specs=(pl.BlockSpec(memory_space=pltpu.VMEM),) * 3,
        scratch_shapes=[
            pltpu.VMEM(coords.shape, f32),
            pltpu.VMEM(velocity.shape, f32),
            pltpu.VMEM(charge.shape, f32),
            pltpu.VMEM(inv_mass.shape, f32),
            pltpu.SMEM(tile_block.shape, i32),
            pltpu.VMEM(tile_atoms.shape, i32),
            pltpu.VMEM(bond_atoms.shape, i32),
            pltpu.VMEM(cross_atoms.shape, i32),
            pltpu.VMEM(cross_side.shape, i32),
            dma((9,)),
            pltpu.VMEM((8, atoms), f32),
            pltpu.VMEM((8, atoms), f32),
            pltpu.VMEM((4, 8, TILE), f32),
            pltpu.VMEM((2, 8, TILE), f32),
            pltpu.VMEM((6, 4, 8, TILE), f32),
            pltpu.VMEM((16, TILE), i32),
            pltpu.VMEM((4, 16, TILE), i32),
            pltpu.VMEM((8, 8, TILE), f32),
            pltpu.VMEM((8, 8, TILE), i32),
            pltpu.VMEM((2, 4, 2 * TILE, DEPTH), bf16),
            pltpu.VMEM((2 * TILE, atoms), bf16),
            pltpu.VMEM((4, 2 * TILE, 2 * TILE), bf16),
            pltpu.VMEM((5, 5 * TILE, 2 * TILE), bf16),
            pltpu.VMEM((3, 2, 8, TILE), f32),
            pltpu.VMEM((3, 4, 2, 8, TILE), f32),
            pltpu.VMEM((2, 8, 8, TILE), f32),
            dma((6,)),
            dma((6,)),
            dma((4,)),
            dma((4,)),
            dma((8,)),
            dma((8,)),
            dma((8,)),
            dma((8,)),
            dma((3, 4)),
            dma((3, 4)),
            dma((2, 8)),
            dma((2, 8)),
        ],
        compiler_params=pltpu.CompilerParams(collective_id=0, has_side_effects=True),
    )(coords, velocity, charge, inv_mass, tile_block, tile_atoms, active_tile_count, bond_atoms, cross_atoms, cross_side, cross_count)
    return moved - correction, velocity_half - correction / time_step


def solution(mesh):
    return jax.shard_map(
        shards,
        mesh=mesh,
        in_specs=(
            P(None, "slab", "dom", None),
            P(None, "slab", "dom", None),
            P("slab", "dom", None),
            P("slab", "dom", None),
            P("slab", "dom", None),
            P("slab", "dom", None, None),
            P("slab", "dom"),
            P(None, "slab", "dom", None),
            P(None, "slab", "dom", None),
            P("slab", "dom", None),
            P("slab", "dom"),
        ),
        out_specs=(P(None, "slab", "dom", None), P(None, "slab", "dom", None)),
        check_vma=False,
    )
```

```python
import functools

import jax
import jax.numpy as jnp
from jax import lax
from jax.experimental import pallas as pl
from jax.experimental.pallas import tpu as pltpu
from jax.sharding import PartitionSpec as P

TILE = 128

time_step = 0.1
cutoff_sq = 16.0
force_scale = 4.0
length_floor = 0.25

MESH = pl.DeviceIdType.MESH
f32, bf16, i32 = jnp.float32, jnp.bfloat16, jnp.int32

FOURTH = 3
DEPTH = 80
TWO_STEPS = ((0, 0), (1, 1), (2, 2), (3, 3), (0, 2), (0, 3), (1, 2), (1, 3))


def parts3(a):
    high = a.astype(bf16).astype(f32)
    rest = a - high
    mid = rest.astype(bf16).astype(f32)
    low = (rest - mid).astype(bf16).astype(f32)
    return high, mid, low


def lanes(table, index):
    return jnp.take_along_axis(table, index, axis=1, mode="promise_in_bounds")


def row_ids():
    return lax.broadcasted_iota(i32, (8, TILE), 0)


def packed(low, high):
    return jnp.where(row_ids() < 4, low, pltpu.roll(high, 4, 0))


def pack_field(field, halves=2):
    parts = [field[:, g * TILE : (g + 1) * TILE] for g in range(2 * halves)]
    return [packed(a, b) for a, b in zip(parts[::2], parts[1::2])]


def half(picked, group):
    return jnp.where((group & 1) == 1, pltpu.roll(picked, 4, 0), picked)


def from_packed(tables, index):
    low, group = index & (TILE - 1), index >> 7
    picked = lanes(tables[0], low)
    for k in range(1, len(tables)):
        picked = jnp.where((group >> 1) == k, lanes(tables[k], low), picked)
    return half(picked, group)


def spread_row(row):
    return jnp.broadcast_to(row, (8, TILE))


def direction(first, second, mask):
    offset = jnp.where(row_ids() < 3, first - second, 0.0)
    squared = jnp.sum(offset * offset, axis=0, keepdims=True)
    masses = (first + second)[FOURTH : FOURTH + 1, :]
    return offset * (lax.rsqrt(squared + length_floor) * lax.rsqrt(masses) * mask)


def project(scaled_dir, first, second):
    return jnp.sum(scaled_dir * (first - second), axis=0, keepdims=True)


def marks(index, atom_ids):
    return jnp.where(jnp.transpose(index.astype(f32))[:, 0:1] == atom_ids, 1.0, 0.0)


class Domain:
    def __init__(self, bonds, slots, far_slots, own_geo, far_geo, bond_inc, cross_inc):
        self.bond_inc, self.cross_inc = bond_inc, cross_inc
        atom_ids = lax.broadcasted_iota(i32, (TILE, bond_inc.shape[1]), 1).astype(f32)
        self.bond_ends = []
        for g in range(2):
            ends = [spread_row(bonds[2 * e + g : 2 * e + g + 1, :]) for e in range(2)]
            self.bond_ends.append(ends)
            bond_inc[g * TILE : (g + 1) * TILE, :] = (
                marks(ends[0], atom_ids) - marks(ends[1], atom_ids)
            ).astype(bf16)
        self.sides = spread_row(slots[2:3, :])
        self.cross_own, self.cross_far, masks = [], [], []
        for n, table in enumerate([slots] + far_slots):
            mine, theirs = (0, 1) if n == 0 else (1, 0)
            self.cross_own.append(spread_row(table[mine : mine + 1, :]))
            self.cross_far.append(spread_row(table[theirs : theirs + 1, :]))
            code = table[2:3, :]
            alive = code < 4 if n == 0 else code == ((n - 1) ^ 1)
            masks.append(jnp.where(alive, 1.0, 0.0))
            cross_inc[n * TILE : (n + 1) * TILE, :] = marks(
                self.cross_own[-1], atom_ids[:, : 2 * TILE]
            ).astype(bf16)
        ones = jnp.ones((1, TILE), f32)
        self.dirs = [
            direction(a, b, m)
            for (a, b), m in zip(
                self.bond_fields(own_geo) + self.cross_fields(own_geo, far_geo), [ones, ones] + masks
            )
        ]

    def bond_fields(self, own):
        return [(from_packed(own, a), from_packed(own, b)) for a, b in self.bond_ends]

    def cross_fields(self, own, far):
        here = [from_packed(own[:1], c) for c in self.cross_own]
        low, group = self.cross_far[0] & (TILE - 1), self.cross_far[0] >> 7
        picked = lanes(far[0], low)
        for k in range(1, 4):
            picked = jnp.where(self.sides == k, lanes(far[k], low), picked)
        there = [half(picked, group)] + [from_packed([far[k]], self.cross_far[k + 1]) for k in range(4)]
        return list(zip(here, there))

    def bond_changes(self, own):
        return [project(d, a, b) for d, (a, b) in zip(self.dirs[:2], self.bond_fields(own))]

    def cross_changes(self, own, far):
        return [project(d, a, b) for d, (a, b) in zip(self.dirs[2:], self.cross_fields(own, far))]

    def changes(self, own, far):
        return self.bond_changes(own) + self.cross_changes(own, far)

    def spread(self, values):
        pushed = jnp.concatenate([d * v for d, v in zip(self.dirs, values)], axis=1)
        high = pushed.astype(bf16).astype(f32)
        pushed = jnp.concatenate([high, pushed - high], axis=0).astype(bf16)
        bonds = jnp.dot(pushed[:, : 2 * TILE], self.bond_inc[...], preferred_element_type=f32)
        cross = jnp.dot(pushed[:, 2 * TILE :], self.cross_inc[...], preferred_element_type=f32)
        total = bonds[:, : 2 * TILE] + cross
        if bonds.shape[1] > 2 * TILE:
            total = jnp.concatenate([total, bonds[:, 2 * TILE :]], axis=1)
        return total[:8] + total[8:]


def kernel(
    n_slab,
    n_dom,
    coords_hbm,
    velocity_hbm,
    charge_hbm,
    mass_hbm,
    block_hbm,
    atoms_hbm,
    live_ref,
    bond_hbm,
    cross_hbm,
    side_hbm,
    cross_count_ref,
    moved_ref,
    velocity_half_ref,
    correction_ref,
    coords_ref,
    velocity_ref,
    charge_ref,
    mass_ref,
    block_ref,
    atoms_ref,
    bond_ref,
    cross_ref,
    side_ref,
    load_sem,
    own_ref,
    speed_ref,
    rim_ref,
    inner_ref,
    rims_ref,
    index_ref,
    indices_ref,
    geo2_ref,
    slots2_ref,
    near_ref,
    bond_inc_ref,
    ghost_bond_inc_ref,
    cross_inc_ref,
    field_ref,
    fields_ref,
    fields2_ref,
    rim_send,
    rim_recv,
    index_send,
    index_recv,
    geo2_send,
    geo2_recv,
    slots2_send,
    slots2_recv,
    field_send,
    field_recv,
    field2_send,
    field2_recv,
):
    slab, dom = lax.axis_index("slab"), lax.axis_index("dom")
    width = max(2, n_dom // 8)
    strides = (1, -1, width, -width)

    def holder(stride):
        return slab, lax.rem(dom + 2 * n_dom - stride, n_dom)

    in_slab = [holder(s) for s in strides]
    across = [(lax.rem(slab + n_slab + s, n_slab), dom) for s in (1, -1)]
    beyond = [holder(strides[a] + strides[b]) for a, b in TWO_STEPS]
    targets = in_slab + across

    barrier = pltpu.get_barrier_semaphore()
    for target in targets:
        pl.semaphore_signal(barrier, inc=1, device_id=target, device_id_type=MESH)

    loads = [
        pltpu.make_async_copy(src, dst, load_sem.at[n])
        for n, (src, dst) in enumerate(
            (
                (coords_hbm, coords_ref),
                (charge_hbm, charge_ref),
                (mass_hbm, mass_ref),
                (cross_hbm, cross_ref),
                (side_hbm, side_ref),
                (bond_hbm, bond_ref),
                (velocity_hbm, velocity_ref),
                (block_hbm, block_ref),
                (atoms_hbm, atoms_ref),
            )
        )
    ]
    for load in loads:
        load.start()
    for load in loads[:6]:
        load.wait()

    for c in range(3):
        own_ref[c : c + 1, :] = coords_ref[c, 0]
        own_ref[4 + c : 5 + c, :] = coords_ref[c, 0]
    own_ref[3:4, :] = mass_ref[0]
    own_ref[7:8, :] = charge_ref[0]
    own = own_ref[...]
    rows = lax.broadcasted_iota(i32, own.shape, 0)
    parts = [own[:, g * TILE : (g + 1) * TILE] for g in range(4)]
    geo = [packed(parts[0], parts[1]), packed(parts[2], parts[3])]
    pair_tables = [jnp.where(row_ids() < 4, pltpu.roll(p, 4, 0), p) for p in parts]
    for g in range(2):
        rim_ref[g] = pair_tables[g]
        rim_ref[2 + g] = geo[g]
        inner_ref[g] = pair_tables[2 + g]
    index_ref[...] = jnp.zeros_like(index_ref)
    index_ref[0:1, :] = cross_ref[0, 0]
    index_ref[1:2, :] = cross_ref[1, 0]
    slot_ids = lax.broadcasted_iota(i32, (1, TILE), 1)
    index_ref[2:3, :] = jnp.where(slot_ids < cross_count_ref[...], side_ref[0], 8)
    for e in range(2):
        for g in range(2):
            row = 8 + 2 * e + g
            index_ref[row : row + 1, :] = bond_ref[e, 0][:, g * TILE : (g + 1) * TILE]

    copies = []

    def send(src, dst, sent, landed, target):
        copy = pltpu.make_async_remote_copy(
            src_ref=src, dst_ref=dst, send_sem=sent, recv_sem=landed, device_id=target, device_id_type=MESH
        )
        copy.start()
        copies.append(copy)
        return copy

    pl.semaphore_wait(barrier, len(targets))
    rims = []
    for n, target in enumerate(targets):
        size = 2
        rims.append(send(rim_ref.at[pl.ds(0, size)], rims_ref.at[n, pl.ds(0, size)], rim_send.at[n], rim_recv.at[n], target))
    shells = [
        send(rim_ref.at[pl.ds(2, 2)], rims_ref.at[n, pl.ds(2, 2)], rim_send.at[6 + n], rim_recv.at[6 + n], target)
        for n, target in enumerate(in_slab)
    ]
    indices = [
        send(index_ref, indices_ref.at[n], index_send.at[n], index_recv.at[n], target)
        for n, target in enumerate(in_slab)
    ]

    norm = own[0:1, :] * own[0:1, :] + own[1:2, :] * own[1:2, :] + own[2:3, :] * own[2:3, :]
    zeros = jnp.zeros_like(own)
    distance = parts3(jnp.where(rows < 3, (-2.0 / cutoff_sq) * own, 0.0))
    charges = parts3(jnp.where(rows == 3, 2.0 * force_scale * pltpu.roll(own, 4, 0), 0.0))
    norms = parts3((norm + 1.0) * (1.0 / cutoff_sq))
    for which in range(2):
        constant = jnp.where(rows == 4 * which, 1.0 / cutoff_sq, 0.0)
        tails = [[jnp.where(rows == FOURTH, k, constant) for k in norms] + [zeros], [zeros] * 4]
        for at, ((h, m, l), tail) in enumerate(zip((distance, charges), tails)):
            pieces = [h, m, l, h, m, h]
            if which:
                pieces = [pltpu.roll(p, 4, 0) for p in pieces]
            near = jnp.transpose(jnp.concatenate(pieces + tail, axis=0)).astype(bf16)
            for b in range(4):
                near_ref[which, b, at * TILE : (at + 1) * TILE, :] = near[b * TILE : (b + 1) * TILE, :]

    for copy in rims:
        copy.wait_recv()
    geo2, slots2 = [], []
    for n, target in enumerate(beyond):
        geo2.append(send(rim_ref.at[2], geo2_ref.at[n], geo2_send.at[n], geo2_recv.at[n], target))
        slots2.append(send(index_ref.at[pl.ds(0, 8)], slots2_ref.at[n], slots2_send.at[n], slots2_recv.at[n], target))

    for load in loads[6:]:
        load.wait()

    n_tiles = atoms_ref.shape[2]

    def gather():
        index = atoms_ref[0, 0]
        fars = []
        tables = [rim_ref[0], rim_ref[1], inner_ref[0], inner_ref[1]]
        tables += [rims_ref[n, g] for n in range(6) for g in range(2)]
        ids = row_ids()
        for r in range(n_tiles // 2):
            entry = jnp.where(ids < 4, spread_row(index[2 * r : 2 * r + 1, :]), spread_row(index[2 * r + 1 : 2 * r + 2, :]))
            low = entry & (TILE - 1)
            found = [lanes(t, low) for t in tables]
            for bit in range(4):
                upper = (entry & (TILE << bit)) != 0
                found = [jnp.where(upper, b, a) for a, b in zip(found[::2], found[1::2])]
            found = found[0]
            h, m, l = parts3(found)
            fourth = (ids & 3) == FOURTH
            square = jnp.where(fourth, 0.0, found * found)
            square = square + pltpu.roll(square, 7, 0) + pltpu.roll(square, 6, 0)
            squares = [jnp.where(ids == FOURTH, 1.0, s) for s in parts3(square)]
            far = jnp.concatenate([h, h, h, m, m, l] + squares + [jnp.zeros_like(h)], axis=0).astype(bf16)
            far2 = jnp.concatenate([jnp.where(fourth, 1.0, h), jnp.where(fourth, 0.0, m)], axis=0).astype(bf16)
            fars += [far, far2]
        return tuple(fars)

    live = live_ref[...]

    def pairs(fars):
        totals = [jnp.zeros((8, TILE), f32) for _ in range(8)]
        for r in range(n_tiles // 2):
            far, far2 = fars[2 * r : 2 * r + 2]
            blocks = [block_ref[0, 0, 2 * r + which] for which in range(2)]
            near = jnp.concatenate([near_ref[which, blocks[which]] for which in range(2)], axis=0)
            both = jnp.dot(near, far, preferred_element_type=f32)
            for which, block in enumerate(blocks):
                tile = 2 * r + which
                dist, charge = (both[k * TILE : (k + 1) * TILE] for k in (2 * which, 2 * which + 1))
                inverse = 1.0 / dist
                edge = inverse * jnp.maximum((1.0 + 1.0 / cutoff_sq) - dist, 0.0)
                strength = (inverse - charge) * (edge * edge)
                high = strength.astype(bf16)
                rest = (strength - high.astype(f32)).astype(bf16)
                summed = lax.dot_general(
                    far2,
                    jnp.concatenate([high, rest], axis=0),
                    (((1,), (1,)), ((), ())),
                    preferred_element_type=f32,
                )
                summed = summed[:, :TILE] + summed[:, TILE:]
                summed = summed[:8] + summed[8:]
                summed = summed * jnp.where(tile < live, 1.0, 0.0)
                for b in range(4):
                    weight = jnp.where(block == b, 1, 0).astype(f32)
                    totals[4 * which + b] = totals[4 * which + b] + summed * weight
        return totals

    totals = pairs(gather())
    totals = [packed_sum(a, b) for a, b in zip(totals[:4], totals[4:])]
    totals = jnp.concatenate(totals, axis=1) * (1.0 / 512.0)
    speed_ref[...] = jnp.zeros_like(speed_ref)
    for c in range(3):
        speed_ref[c : c + 1, :] = velocity_ref[c, 0]
    mass = own[3:4, :]
    force = jnp.where(rows < 3, own * totals[FOURTH : FOURTH + 1, :] - totals, 0.0)
    velocity_half = speed_ref[...] + time_step * force * mass
    displace = time_step * velocity_half
    moved = own + displace

    def exchange(step, tables):
        for g, table in enumerate(tables):
            field_ref[step, g] = table
        size = len(tables)
        sent = [
            send(
                field_ref.at[step, pl.ds(0, size)],
                fields_ref.at[step, n, pl.ds(0, size)],
                field_send.at[step, n],
                field_recv.at[step, n],
                target,
            )
            for n, target in enumerate(in_slab)
        ]
        if size == 2:
            sent += [
                send(field_ref.at[step, 0], fields2_ref.at[step, n], field2_send.at[step, n], field2_recv.at[step, n], target)
                for n, target in enumerate(beyond)
            ]
        return sent

    def arrive(sent):
        for copy in sent:
            copy.wait_recv()

    def around(n, mine, near_by, two_steps):
        found = []
        for k in range(4):
            pair = (n, k) if (n, k) in TWO_STEPS else (k, n)
            found.append(mine if k == n ^ 1 else two_steps[TWO_STEPS.index(pair)])
        return found

    displaced = pack_field(displace)
    sent = exchange(0, displaced)

    arrive(shells + indices)
    own_index = index_ref[...]
    near_index = [indices_ref[n] for n in range(4)]
    near_geo = [[rims_ref[n, 2], rims_ref[n, 3]] for n in range(4)]
    here = Domain(
        own_index[8:12, :],
        own_index[0:8, :],
        [i[0:8, :] for i in near_index],
        geo,
        [g[0] for g in near_geo],
        bond_inc_ref,
        cross_inc_ref.at[4],
    )
    arrive(geo2 + slots2)
    far_index = [slots2_ref[n] for n in range(8)]
    far_geo = [geo2_ref[n] for n in range(8)]
    ghosts, masses = [], []
    for n in range(4):
        ghosts.append(
            Domain(
                near_index[n][8:12, :],
                near_index[n][0:8, :],
                around(n, own_index[0:8, :], near_index, far_index),
                near_geo[n],
                around(n, geo[0], near_geo, far_geo),
                ghost_bond_inc_ref.at[n],
                cross_inc_ref.at[n],
            )
        )
        first = near_geo[n][0]
        masses.append(jnp.concatenate([first[FOURTH : FOURTH + 1, :], first[4 + FOURTH :, :]], axis=1))

    def ghost_changes(mine, step):
        by = [[fields_ref[step, n, g] for g in range(2)] for n in range(4)]
        two = [fields2_ref[step, n] for n in range(8)]
        return [ghosts[n].changes(by[n], around(n, mine[0], by, two)) for n in range(4)]

    def minus(a, b):
        return [x - y for x, y in zip(a, b)]

    def far_spread(values):
        return [pack_field(g.spread(v) * m, 1)[0] for g, v, m in zip(ghosts, values, masses)]

    local = here.bond_changes(displaced)
    arrive(sent)
    start = local + here.cross_changes(displaced, [fields_ref[0, n, 0] for n in range(4)])
    ghost_start = ghost_changes(displaced, 0)
    field1 = here.spread(start) * mass
    far = far_spread(ghost_start)
    first = minus(start, here.changes(pack_field(field1), far))
    field2 = field1 + here.spread(first) * mass
    both = pack_field(field2)
    sent = exchange(1, both)
    local = here.bond_changes(both)
    arrive(sent)
    second = minus(start, local + here.cross_changes(both, [fields_ref[1, n, 0] for n in range(4)]))
    ghost_second = [minus(a, b) for a, b in zip(ghost_start, ghost_changes(both, 1))]
    field3 = here.spread(second) * mass
    third = minus(second, here.changes(pack_field(field3), far_spread(ghost_second)))
    field4 = pack_field(here.spread(third) * mass)
    sent = exchange(2, field4[:1])
    local = here.bond_changes(field4)
    before = [a + b + c + 2.0 * d for a, b, c, d in zip(start, first, second, third)]
    arrive(sent)
    last = local + here.cross_changes(field4, [fields_ref[2, n, 0] for n in range(4)])
    correction = here.spread(minus(before, last)) * mass
    for c in range(3):
        moved_ref[c, 0] = moved[c : c + 1, :]
        velocity_half_ref[c, 0] = velocity_half[c : c + 1, :]
        correction_ref[c, 0] = correction[c : c + 1, :]
    for copy in copies:
        copy.wait_send()


def packed_sum(first, second):
    return first + pltpu.roll(second, 4, 0)


def shards(coords, velocity, charge, inv_mass, tile_block, tile_atoms, active_tile_count, bond_atoms, cross_atoms, cross_side, cross_count):
    n_slab, n_dom = lax.axis_size("slab"), lax.axis_size("dom")
    atoms = coords.shape[-1]
    tiles = tile_atoms.shape[2]
    shape = jax.ShapeDtypeStruct(coords.shape, f32)
    dma = pltpu.SemaphoreType.DMA
    vmem = pl.BlockSpec(memory_space=pltpu.VMEM)
    moved, velocity_half, correction = pl.pallas_call(
        functools.partial(kernel, n_slab, n_dom),
        out_shape=(pltpu.VMEM(coords.shape, f32),) * 3,
        in_specs=[vmem if n in (6, 10) else pl.BlockSpec(memory_space=pl.ANY) for n in range(11)],
        out_specs=(pl.BlockSpec(memory_space=pltpu.VMEM),) * 3,
        scratch_shapes=[
            pltpu.VMEM(coords.shape, f32),
            pltpu.VMEM(velocity.shape, f32),
            pltpu.VMEM(charge.shape, f32),
            pltpu.VMEM(inv_mass.shape, f32),
            pltpu.SMEM(tile_block.shape, i32),
            pltpu.VMEM(tile_atoms.shape, i32),
            pltpu.VMEM(bond_atoms.shape, i32),
            pltpu.VMEM(cross_atoms.shape, i32),
            pltpu.VMEM(cross_side.shape, i32),
            dma((9,)),
            pltpu.VMEM((8, atoms), f32),
            pltpu.VMEM((8, atoms), f32),
            pltpu.VMEM((4, 8, TILE), f32),
            pltpu.VMEM((2, 8, TILE), f32),
            pltpu.VMEM((6, 4, 8, TILE), f32),
            pltpu.VMEM((16, TILE), i32),
            pltpu.VMEM((4, 16, TILE), i32),
            pltpu.VMEM((8, 8, TILE), f32),
            pltpu.VMEM((8, 8, TILE), i32),
            pltpu.VMEM((2, 4, 2 * TILE, DEPTH), bf16),
            pltpu.VMEM((2 * TILE, atoms), bf16),
            pltpu.VMEM((4, 2 * TILE, 2 * TILE), bf16),
            pltpu.VMEM((5, 5 * TILE, 2 * TILE), bf16),
            pltpu.VMEM((3, 2, 8, TILE), f32),
            pltpu.VMEM((3, 4, 2, 8, TILE), f32),
            pltpu.VMEM((2, 8, 8, TILE), f32),
            dma((10,)),
            dma((10,)),
            dma((4,)),
            dma((4,)),
            dma((8,)),
            dma((8,)),
            dma((8,)),
            dma((8,)),
            dma((3, 4)),
            dma((3, 4)),
            dma((2, 8)),
            dma((2, 8)),
        ],
        compiler_params=pltpu.CompilerParams(collective_id=0, has_side_effects=True),
    )(coords, velocity, charge, inv_mass, tile_block, tile_atoms, active_tile_count, bond_atoms, cross_atoms, cross_side, cross_count)
    return moved - correction, velocity_half - correction / time_step


def solution(mesh):
    return jax.shard_map(
        shards,
        mesh=mesh,
        in_specs=(
            P(None, "slab", "dom", None),
            P(None, "slab", "dom", None),
            P("slab", "dom", None),
            P("slab", "dom", None),
            P("slab", "dom", None),
            P("slab", "dom", None, None),
            P("slab", "dom"),
            P(None, "slab", "dom", None),
            P(None, "slab", "dom", None),
            P("slab", "dom", None),
            P("slab", "dom"),
        ),
        out_specs=(P(None, "slab", "dom", None), P(None, "slab", "dom", None)),
        check_vma=False,
    )
```
